32 devices in a mesh: rep: 8 (over z, y), seq: 4 (over x, core).
Axes of the slice: x: 2, y: 2, z: 4, core: 2. Of those that a mesh axis runs over, the one named last changes fastest.
Arguments:
- inputs: bfloat16 [8, 2048, 2048], P('rep', 'seq'), may hold values from -6 to 6
- query: bfloat16 [8, 2048, 1024], P('rep', 'seq'), may hold values from -6 to 6
- key_feat: bfloat16 [8, 2048, 1024], P('rep', 'seq'), may hold values from -6 to 6
- cotangent: bfloat16 [8, 2048, 2048], P('rep', 'seq'), may hold values from -6 to 6
- value_weight: bfloat16 [8, 2048, 1024], P('rep', 'seq'), may hold values from -6 to 6
- output_weight: bfloat16 [8, 1024, 2048], P('rep', 'seq'), may hold values from -6 to 6
- stale_value: bfloat16 [8, 2048, 1024], P('rep', 'seq'), may hold values from -6 to 6
- stale_output: bfloat16 [8, 1024, 2048], P('rep', 'seq'), may hold values from -6 to 6
- step_counts: int32 [8], replicated, may hold values from 1 to 999
- partner: int32 [8], replicated, may hold values from 0 to 7, as said below
Outputs:
- new_value: bfloat16 [8, 2048, 1024], P('rep', 'seq')
- new_output: bfloat16 [8, 1024, 2048], P('rep', 'seq')
The draws below stay inside these ranges and needn't reach their ends.
Inputs may be any that keep to these rules, and one draw needn't show every extreme that they name: partner pairs the replicas: partner[partner[r]] = r and partner[r] != r for every r.
All inputs are finite; a program needn't handle non-finite values.
Results may differ from the reference program's by a relative error of at most 0.009.
Values may be sent and summed in bfloat16 or wider, within the bound.
A program may use at most 128 MiB of HBM per device.

```python
import jax
import jax.numpy as jnp
from jax import lax

D = 2048
HEADS = 16
HEAD = 64
TOK_DEV = 512
HD = 1024
TOKENS = 2048
REPS = 8
N_SEQ = 4


def draw_partner(key, part):
    order = jax.random.permutation(jax.random.fold_in(key, 7), REPS).astype(jnp.int32)
    paired = order.reshape(REPS // 2, 2)[:, ::-1].reshape(REPS)
    return jnp.zeros((REPS,), jnp.int32).at[order].set(paired)


def place_ends(drawn, key, least, high):
    dims = drawn.shape
    spot = [jax.random.randint(jax.random.fold_in(key, axis), (), 0, dims[axis]) for axis in range(len(dims))]
    drawn = drawn.at[tuple(spot)].set(least)
    longest = dims.index(max(dims))
    spot[longest] = (spot[longest] + 1) % dims[longest]
    return drawn.at[tuple(spot)].set(high)


def block_scale(own_key, extent, cuts, least, top_value):
    loudness, own = 1.0, jax.random.fold_in(own_key, 6)
    for position, blocks in cuts:
        draws = jnp.exp(jax.random.uniform(jax.random.fold_in(own, position), (blocks,), jnp.float32, least / len(cuts), top_value / len(cuts)))
        loudness = loudness * jnp.repeat(draws, extent[position] // blocks).reshape([-1 if axis == position else 1 for axis in range(len(extent))])
    return loudness


def scatter_about(rng, dims, deviation, most, pieces=(), kind=jnp.bfloat16):
    values = deviation * jax.random.normal(rng, dims, jnp.float32)
    if pieces:
        values = values * block_scale(rng, dims, pieces, -0.22, 0.18)
    return jnp.clip(values, -most, most).astype(kind)


def setup_inputs(seed: int = 0) -> dict:
    keys = jax.random.split(jax.random.key(seed), 11)
    inputs = scatter_about(keys[0], (REPS, TOKENS, D), 1.0, 6.0, ((0, 8), (1, 4)))
    query = scatter_about(keys[1], (REPS, TOKENS, HD), 1.0, 6.0, ((0, 8), (1, 4)))
    key_feat = scatter_about(keys[2], (REPS, TOKENS, HD), 1.0, 6.0, ((0, 8), (1, 4)))
    cotangent = scatter_about(keys[3], (REPS, TOKENS, D), 1.0, 6.0, ((0, 8), (1, 4)))
    value_weight = scatter_about(keys[4], (REPS, D, HD), 1.0, 6.0, ((0, 8), (1, 4)))
    output_weight = scatter_about(keys[5], (REPS, HD, D), 1.0, 6.0, ((0, 8), (1, 4)))
    stale_value = scatter_about(keys[6], (REPS, D, HD), 1.0, 6.0, ((0, 8), (1, 4)))
    stale_output = scatter_about(keys[7], (REPS, HD, D), 1.0, 6.0, ((0, 8), (1, 4)))
    step_counts = place_ends(jax.random.randint(keys[8], (REPS,), 1, 1000), jax.random.fold_in(keys[8], 1), 1, 999).astype(jnp.int32)
    partner = draw_partner(jax.random.fold_in(keys[10], 71), 0)
    return {"inputs": inputs, "query": query, "key_feat": key_feat, "cotangent": cotangent, "value_weight": value_weight, "output_weight": output_weight, "stale_value": stale_value, "stale_output": stale_output, "step_counts": step_counts, "partner": partner}


learning_rate = 0.25
norm_eps = 1e-06

def rounded(array):
    return lax.optimization_barrier(array.astype(jnp.bfloat16)).astype(jnp.float32)

def reference(inputs, query, key_feat, cotangent, value_weight, output_weight, stale_value, stale_output, step_counts, partner):
    width = HEADS * HEAD
    scale_value = D ** (-0.5)
    scale_output = width ** (-0.5)
    highest = lax.Precision.HIGHEST
    causal = jnp.arange(TOK_DEV)[:, None] >= jnp.arange(TOK_DEV)[None, :]

    def replica(index):
        mate = partner[index]
        features = inputs[index]
        weight_v = value_weight[index]
        weight_o = output_weight[index]
        upstream_rows = cotangent[index]
        values = rounded(jnp.dot(features, weight_v, preferred_element_type=jnp.float32) * scale_value)
        query_blocks = query[index].astype(jnp.float32).reshape(N_SEQ, TOK_DEV, HEADS, HEAD)
        key_blocks = key_feat[index].astype(jnp.float32).reshape(N_SEQ, TOK_DEV, HEADS, HEAD)
        value_blocks = values.reshape(N_SEQ, TOK_DEV, HEADS, HEAD)
        states = jnp.einsum('bthe,bthf->bhef', key_blocks, value_blocks, precision=highest)
        running = jnp.cumsum(states, axis=0)
        prior = rounded(jnp.concatenate([jnp.zeros_like(states[:1]), running[:-1]], axis=0))
        scores = jnp.einsum('bthe,bshe->bhts', query_blocks, key_blocks, precision=highest)
        scores = rounded(jnp.where(causal, scores, jnp.float32(0.0)))
        attn = jnp.einsum('bhts,bshf->bthf', scores, value_blocks, precision=highest)
        attn = attn + jnp.einsum('bthe,bhef->bthf', query_blocks, prior, precision=highest)
        inverse = lax.rsqrt(lax.optimization_barrier(jnp.mean(attn * attn, axis=-1, keepdims=True)) + norm_eps)
        unit = attn * inverse
        normed = rounded(unit)
        upstream = jnp.dot(upstream_rows, weight_o.T, preferred_element_type=jnp.float32) * scale_output
        upstream = upstream.reshape(N_SEQ, TOK_DEV, HEADS, HEAD)
        d_attn = rounded(inverse * (upstream - unit * lax.optimization_barrier(jnp.mean(unit * upstream, axis=-1, keepdims=True))))
        grad_states = jnp.einsum('bthe,bthf->bhef', query_blocks, d_attn, precision=highest)
        backward = jnp.cumsum(grad_states[::-1], axis=0)[::-1]
        later = rounded(jnp.concatenate([backward[1:], jnp.zeros_like(grad_states[:1])], axis=0))
        d_values = jnp.einsum('bhts,bthf->bshf', scores, d_attn, precision=highest)
        d_values = rounded(d_values + jnp.einsum('bshe,bhef->bshf', key_blocks, later, precision=highest))
        d_values = d_values.reshape(N_SEQ, TOK_DEV, width)
        feature_blocks = features.astype(jnp.float32).reshape(N_SEQ, TOK_DEV, D)
        grad_value = lax.optimization_barrier(jnp.sum(rounded(jnp.einsum('btd,btf->bdf', feature_blocks, d_values, precision=highest) * scale_value), axis=0))
        normed_blocks = normed.reshape(N_SEQ, TOK_DEV, width)
        upstream_blocks = upstream_rows.astype(jnp.float32).reshape(N_SEQ, TOK_DEV, D)
        grad_output = lax.optimization_barrier(jnp.sum(rounded(jnp.einsum('btf,btd->bfd', normed_blocks, upstream_blocks, precision=highest) * scale_output), axis=0))
        own_count = step_counts[index].astype(jnp.float32)
        mate_count = step_counts[mate].astype(jnp.float32)
        mix = mate_count / (own_count + mate_count)
        new_value = (1.0 - mix) * weight_v.astype(jnp.float32) + mix * stale_value[mate].astype(jnp.float32) - learning_rate * grad_value
        new_output = (1.0 - mix) * weight_o.astype(jnp.float32) + mix * stale_output[mate].astype(jnp.float32) - learning_rate * grad_output
        return (new_value.astype(jnp.bfloat16), new_output.astype(jnp.bfloat16))
    new_value, new_output = lax.map(replica, jnp.arange(REPS, dtype=jnp.int32))
    return (new_value, new_output)
```

```python
import functools

import jax
import jax.numpy as jnp
from jax import lax
from jax.experimental import pallas as pl
from jax.experimental.pallas import tpu as pltpu
from jax.sharding import PartitionSpec as P

HEAD = 64
PAIR = 2 * HEAD
learning_rate = 0.25
norm_eps = 1e-06
F32 = jnp.float32
BF16 = jnp.bfloat16
TN = (((0,), (0,)), ((), ()))
NT = (((1,), (1,)), ((), ()))
CHUNKS = 2


def dot(a, b, dims=(((1,), (0,)), ((), ()))):
    return lax.dot_general(a, b, dims, preferred_element_type=F32)


def kernel(
    reps, row_parts,
    x_hbm, q_hbm, k_hbm, c_hbm, wv_hbm, wo_hbm, sv_hbm, so_hbm, counts, partner,
    nv_ref, no_ref,
    x, q, k, c, wv, wo, scores, acc, values, inv, normed, upstream, d_attn,
    spread_v, spread_o, pick_v, pick_o, mate_v, mate_o,
    state_own, state_sib, state_chip, state_far,
    later_own, later_sib, later_chip, later_far,
    part_o, sib_o, sum_o, far_o, part_v, sib_v, sum_v, far_v,
    load_sem, send_sem, recv_sem, spread_send, spread_recv, mate_send, mate_recv,
):
    rep = lax.axis_index("rep")
    me = lax.axis_index("seq")
    core = lax.rem(me, 2)
    chip = me // 2
    sib = chip * 2 + 1 - core
    far = (1 - chip) * 2 + core
    diag = (1 - chip) * 2 + 1 - core
    positions, depth = x.shape
    width = q.shape[1]
    half = positions // 2
    pairs = width // PAIR
    scale_value = depth ** (-0.5)
    scale_output = width ** (-0.5)
    used = [0]

    def remote(src, dst, target):
        index = used[0]
        used[0] += 1
        return pltpu.make_async_remote_copy(
            src_ref=src, dst_ref=dst, send_sem=send_sem.at[index], recv_sem=recv_sem.at[index],
            device_id={"seq": target}, device_id_type=pl.DeviceIdType.MESH,
        )

    barrier = pltpu.get_barrier_semaphore()
    for target in (sib, far):
        pl.semaphore_signal(
            barrier, inc=1, device_id={"seq": target}, device_id_type=pl.DeviceIdType.MESH
        )

    @pl.loop(1, reps)
    def _(step):
        pl.semaphore_signal(
            barrier, inc=1, device_id={"rep": lax.rem(rep + step, reps)},
            device_id_type=pl.DeviceIdType.MESH,
        )

    loads = [
        pltpu.make_async_copy(src, dst, load_sem.at[index])
        for index, (src, dst) in enumerate(
            ((q_hbm, q), (k_hbm, k), (wv_hbm, wv.at[me]), (x_hbm, x), (wo_hbm, wo.at[me]), (c_hbm, c))
        )
    ]
    for copy in loads:
        copy.start()
    pl.semaphore_wait(barrier, reps + 1)

    def split(rows):
        return [pl.ds(i * (rows // CHUNKS), rows // CHUNKS) for i in range(CHUNKS)]

    rows_v, rows_o = split(wv.shape[1]), split(wo.shape[1])
    far_wv = [remote(wv_hbm.at[r], wv.at[me, r], far) for r in rows_v]
    sib_wv = remote(wv_hbm, wv.at[me], sib)
    far_wo = [remote(wo_hbm.at[r], wo.at[me, r], far) for r in rows_o]
    sib_wo = remote(wo_hbm, wo.at[me], sib)
    pass_wv = [remote(wv.at[far, r], wv.at[far, r], sib) for r in rows_v]
    pass_wo = [remote(wo.at[far, r], wo.at[far, r], sib) for r in rows_o]
    for copy in far_wv:
        copy.start()
    sib_wv.start()
    far_wo[0].start()
    sib_wo.start()

    col_parts = reps // row_parts
    high_v, wide_v = spread_v.shape[1:]
    high_o, wide_o = spread_o.shape[1:]

    def place(index, high, wide):
        row = pl.multiple_of((index // col_parts) * high, high)
        column = pl.multiple_of(lax.rem(index, col_parts) * wide, wide)
        return pl.ds(row, high), pl.ds(column, wide)

    def piece(ref, index, high, wide):
        rows, columns = place(index, high, wide)
        return ref.at[rows, columns]

    sources = (sv_hbm, so_hbm)
    spreads = (spread_v, spread_o)
    picks = (pick_v, pick_o)
    mates = (mate_v, mate_o)
    extents = ((high_v, wide_v), (high_o, wide_o))

    side = reps // 2
    high, low = rep // side, lax.rem(rep, side)

    def exchange(step, kind, which):
        near = step // side
        group = high * near + (1 - high) * (1 - near)
        hop = step - near * (side - 1)
        target = group * side + lax.rem(low // 2 + hop // 2, side // 2) * 2 + lax.rem(low + hop, 2)
        if which == 0:
            src, dst = piece(sources[kind], target, *extents[kind]), spreads[kind]
            sems = (spread_send, spread_recv)
        else:
            src, dst = picks[kind].at[target], mates[kind]
            sems = (mate_send, mate_recv)
        return pltpu.make_async_remote_copy(
            src_ref=src, dst_ref=dst.at[rep], send_sem=sems[0].at[kind, step],
            recv_sem=sems[1].at[kind, step], device_id={"rep": target},
            device_id_type=pl.DeviceIdType.MESH,
        )

    def run_exchange(kind, which, act):
        @pl.loop(0, reps - 1)
        def _(step):
            act(exchange(step, kind, which))

    run_exchange(0, 0, lambda copy: copy.start())
    own_pieces = [
        pltpu.make_async_copy(piece(sv_hbm, rep, high_v, wide_v), spread_v.at[rep], load_sem.at[6]),
        pltpu.make_async_copy(piece(so_hbm, rep, high_o, wide_o), spread_o.at[rep], load_sem.at[7]),
    ]
    for copy in own_pieces:
        copy.start()

    mate = partner[rep]

    def pick(kind):
        own_pieces[kind].wait()
        run_exchange(kind, 0, lambda copy: copy.wait())

        @pl.loop(0, reps)
        def _(r):
            picks[kind][r] = spreads[kind][partner[r]]

        run_exchange(kind, 1, lambda copy: copy.start())
        mates[kind][rep] = spreads[kind][mate]

    def lanes(p):
        return pl.ds(pl.multiple_of(p * PAIR, PAIR), PAIR)

    def first_lanes(rows):
        return lax.broadcasted_iota(jnp.int32, (rows, PAIR), 1) < HEAD

    def diagonal():
        row = lax.broadcasted_iota(jnp.int32, (PAIR, PAIR), 0) < HEAD
        column = lax.broadcasted_iota(jnp.int32, (PAIR, PAIR), 1) < HEAD
        return row == column

    loads[0].wait()
    loads[1].wait()

    @pl.loop(0, pairs)
    def _(p):
        keys = k[:, lanes(p)]
        queries = q[:, lanes(p)]
        first = first_lanes(positions)
        zero = jnp.zeros_like(queries)
        causal = lax.broadcasted_iota(jnp.int32, (half, half), 0) >= lax.broadcasted_iota(
            jnp.int32, (half, half), 1
        )
        for h in range(2):
            mine = jnp.where(first, queries, zero) if h == 0 else jnp.where(first, zero, queries)
            head = p * 2 + h
            low = dot(mine[half:], keys[:half], NT)
            scores[head, half:, :half] = low.astype(BF16)
            for b in range(2):
                block = slice(b * half, (b + 1) * half)
                square = dot(mine[block], keys[block], NT)
                scores[head, block, block] = jnp.where(causal, square, 0.0).astype(BF16)

    tile = 256

    def add_values(block, begin):
        columns = pl.ds(pl.multiple_of(block * wv.shape[1], wv.shape[1]), wv.shape[1])

        @pl.loop(0, width // tile)
        def _(n):
            out = pl.ds(pl.multiple_of(n * tile, tile), tile)
            term = dot(x[:, columns], wv[block, :, out])
            acc[:, out] = term if begin else acc[:, out] + term

    def add_upstream(block):
        rows = wo.shape[1]
        upstream[:, pl.ds(pl.multiple_of(block * rows, rows), rows)] = (
            dot(c[...], wo[block], NT) * scale_output
        )

    loads[2].wait()
    loads[3].wait()
    add_values(me, True)
    sib_wv.wait()
    add_values(sib, False)
    loads[4].wait()
    loads[5].wait()
    add_upstream(me)
    sib_wo.wait()
    add_upstream(sib)
    for arrive, forward in zip(far_wv, pass_wv):
        arrive.wait()
        forward.start()
    run_exchange(1, 0, lambda copy: copy.start())
    add_values(far, False)
    for forward in pass_wv:
        forward.wait()
    add_values(diag, False)

    @pl.loop(0, width // tile)
    def _(n):
        out = pl.ds(pl.multiple_of(n * tile, tile), tile)
        values[:, out] = (acc[:, out] * scale_value).astype(BF16)

    def states(left, right, own):
        @pl.loop(0, pairs // 2)
        def _(j):
            same = diagonal()
            terms = [
                dot(left[:, lanes(2 * j + i)], right[:, lanes(2 * j + i)], TN) for i in range(2)
            ]
            own[j] = jnp.where(same, terms[0], pltpu.roll(jnp.where(same, terms[1], 0.0), HEAD, 1))

    def unpack(packed, i):
        same = diagonal()
        if i == 0:
            return jnp.where(same, packed, 0.0)
        return pltpu.roll(jnp.where(same, 0.0, packed), HEAD, 1)

    def chip_share(total, landed, sender):
        count = total.shape[0] // 2
        mine = pl.ds(core * count, count)
        cross = remote(total.at[mine], landed.at[mine], far)
        across = remote(landed.at[mine], landed.at[mine], sib)

        def start():
            @pl.when(chip == sender)
            def _():
                landed[...] = jnp.zeros_like(landed)
                cross.start()

        def wait():
            @pl.when(chip == sender)
            def _():
                cross.wait_send()

            @pl.when(chip != sender)
            def _():
                cross.wait_recv()
                across.start()
                across.wait()

        return start, wait

    states(k, values, state_own)
    to_sib = remote(state_own, state_sib, sib)
    to_far = chip_share(state_chip, state_far, 0)
    to_sib.start()
    to_sib.wait()
    state_chip[...] = (state_own[...] + state_sib[...]).astype(BF16)
    to_far[0]()
    far_wo[1].start()

    @pl.loop(0, pairs // 2)
    def _(p2):
        for i in range(2):
            p = p2 * 2 + i
            right = values[:, lanes(p)]
            first = first_lanes(half)
            for b in range(2):
                rows = slice(b * half, (b + 1) * half)
                both = [dot(scores[p * 2 + h, rows, : (b + 1) * half], right[: (b + 1) * half]) for h in range(2)]
                acc[rows, lanes(p)] = jnp.where(first, both[0], both[1])

    to_far[1]()
    after_core = (core == 1).astype(F32)
    after_chip = (chip == 1).astype(F32)

    def head_mean(array, first):
        low = jnp.sum(jnp.where(first, array, 0.0), axis=1, keepdims=True)
        high = jnp.sum(jnp.where(first, 0.0, array), axis=1, keepdims=True)
        return jnp.where(first, low, high) * (1.0 / HEAD)

    @pl.loop(0, pairs // 2)
    def _(j):
        packed = after_core * state_sib[j] + after_chip * state_far[j].astype(F32)
        first = first_lanes(positions)
        for i in range(2):
            span = lanes(2 * j + i)
            prior = unpack(packed, i).astype(BF16)
            attn = acc[:, span] + dot(q[:, span], prior)
            inverse = lax.rsqrt(head_mean(attn * attn, first) + norm_eps)
            unit = attn * inverse
            acc[:, span] = unit
            inv[:, span] = inverse
            normed[:, span] = unit.astype(BF16)

    def tile_o(slot, dest):
        rows = part_o.shape[1]
        left = normed[:, pl.ds(pl.multiple_of(dest * rows, rows), rows)]
        step = depth // 4

        @pl.loop(0, 4)
        def _(n):
            out = pl.ds(pl.multiple_of(n * step, step), step)
            part_o[slot, :, out] = (dot(left, c[:, out], TN) * scale_output).astype(BF16)

    def tile_v(slot, dest):
        rows = part_v.shape[1]

        @pl.loop(0, width // tile)
        def _(n):
            out = pl.ds(pl.multiple_of(n * tile, tile), tile)
            left = x[:, pl.ds(pl.multiple_of(dest * rows, rows), rows)]
            part_v[slot, :, out] = (dot(left, values[:, out], TN) * scale_value).astype(BF16)

    def scatter(make_tile, part, from_sib, total, landed):
        rows = split(part.shape[1])
        pair_far = remote(part.at[0], from_sib.at[0], sib)
        pair_near = remote(part.at[2], from_sib.at[1], sib)
        cross = [remote(total.at[r], landed.at[r], far) for r in rows]
        make_tile(0, diag)
        pair_far.start()
        make_tile(1, far)
        pair_far.wait()
        total[...] = (part[1].astype(F32) + from_sib[0].astype(F32)).astype(BF16)
        return pair_near, cross

    near_o, cross_o = scatter(tile_o, part_o, sib_o, sum_o, far_o)
    cross_o[0].start()
    pick(0)
    for arrive, forward in zip(far_wo, pass_wo):
        arrive.wait()
        forward.start()
    add_upstream(far)
    for forward in pass_wo:
        forward.wait()
    add_upstream(diag)

    @pl.loop(0, pairs)
    def _(p):
        span = lanes(p)
        first = first_lanes(positions)
        up = upstream[:, span]
        unit = acc[:, span]
        d_attn[:, span] = (inv[:, span] * (up - unit * head_mean(unit * up, first))).astype(BF16)

    states(q, d_attn, later_own)
    later_to_sib = remote(later_own, later_sib, sib)
    later_to_far = chip_share(later_chip, later_far, 1)
    later_to_sib.start()
    later_to_sib.wait()
    later_chip[...] = (later_own[...] + later_sib[...]).astype(BF16)
    later_to_far[0]()
    cross_o[1].start()
    pick(1)

    @pl.loop(0, pairs)
    def _(p):
        right = d_attn[:, lanes(p)]
        first = first_lanes(half)
        for b in range(2):
            rows = slice(b * half, (b + 1) * half)
            both = [dot(scores[p * 2 + h, b * half :, rows], right[b * half :], TN) for h in range(2)]
            acc[rows, lanes(p)] = jnp.where(first, both[0], both[1])

    later_to_far[1]()
    before_core = (core == 0).astype(F32)
    before_chip = (chip == 0).astype(F32)

    @pl.loop(0, pairs // 2)
    def _(j):
        packed = before_core * later_sib[j] + before_chip * later_far[j].astype(F32)
        for i in range(2):
            span = lanes(2 * j + i)
            later = unpack(packed, i).astype(BF16)
            values[:, span] = (acc[:, span] + dot(k[:, span], later)).astype(BF16)

    near_v, cross_v = scatter(tile_v, part_v, sib_v, sum_v, far_v)
    for copy in cross_v:
        copy.start()
    tile_o(2, sib)
    near_o.start()
    tile_o(3, me)
    tile_v(2, sib)
    near_v.start()
    tile_v(3, me)

    own_count = counts[rep].astype(F32)
    mate_count = counts[mate].astype(F32)
    share = jnp.full((1, 128), mate_count, F32) / jnp.full((1, 128), own_count + mate_count, F32)
    mix = share[0:1, 0:1]

    run_exchange(0, 1, lambda copy: copy.wait())
    near_v.wait()

    def finish(out, weight, theirs, part, from_sib, landed, high, wide, begin, end):
        @pl.loop(begin, end)
        def _(index):
            at = place(index, high, wide)
            grad = part[(3, *at)].astype(F32) + from_sib[(1, *at)].astype(F32) + landed[at].astype(F32)
            mixed = (1.0 - mix) * weight[(me, *at)].astype(F32) + mix * theirs[index].astype(F32)
            out[at] = (mixed - learning_rate * grad).astype(BF16)

    for i, copy in enumerate(cross_v):
        copy.wait()
        finish(
            nv_ref, wv, mates[0], part_v, sib_v, far_v, high_v, wide_v,
            i * reps // CHUNKS, (i + 1) * reps // CHUNKS,
        )
    near_o.wait()
    for copy in cross_o:
        copy.wait()
    run_exchange(1, 1, lambda copy: copy.wait())
    finish(no_ref, wo, mates[1], part_o, sib_o, far_o, high_o, wide_o, 0, reps)


def hand_over(*refs):
    sources, results, held, sems = refs[:2], refs[2:4], refs[4:6], refs[6]
    fetch, put = [], []
    for kind in range(2):
        step = sources[kind].shape[0] // CHUNKS
        for i in range(CHUNKS):
            rows = pl.ds(i * step, step)
            index = kind * CHUNKS + i
            fetch.append(pltpu.make_async_copy(sources[kind].at[rows], held[kind].at[rows], sems.at[0, index]))
            put.append(pltpu.make_async_copy(held[kind].at[rows], results[kind].at[rows], sems.at[1, index]))
    for copy in fetch:
        copy.start()
    for before, after in zip(fetch, put):
        before.wait()
        after.start()
    for copy in put:
        copy.wait()


def on_device(
    inputs, query, key_feat, cotangent, value_weight, output_weight, stale_value, stale_output,
    step_counts, partner,
):
    arrays = [
        a[0] for a in (inputs, query, key_feat, cotangent, value_weight, output_weight, stale_value, stale_output)
    ]
    reps = lax.axis_size("rep")
    seqs = lax.axis_size("seq")
    positions, depth = arrays[0].shape
    width = arrays[1].shape[1]
    rows_v, rows_o = arrays[4].shape[0], arrays[5].shape[0]
    row_parts = min(reps, 8)
    col_parts = reps // row_parts
    piece_v = (reps, rows_v // row_parts, width // col_parts)
    piece_o = (reps, rows_o // row_parts, depth // col_parts)
    packed = (width // PAIR // 2, PAIR, PAIR)
    vmem = pltpu.VMEM
    scratch = [
        vmem((positions, depth), BF16),
        vmem((positions, width), BF16),
        vmem((positions, width), BF16),
        vmem((positions, depth), BF16),
        vmem((seqs, rows_v, width), BF16),
        vmem((seqs, rows_o, depth), BF16),
        vmem((width // HEAD, positions, positions), BF16),
        vmem((positions, width), F32),
        vmem((positions, width), BF16),
        vmem((positions, width), F32),
        vmem((positions, width), BF16),
        vmem((positions, width), F32),
        vmem((positions, width), BF16),
        vmem(piece_v, BF16), vmem(piece_o, BF16),
        vmem(piece_v, BF16), vmem(piece_o, BF16),
        vmem(piece_v, BF16), vmem(piece_o, BF16),
        vmem(packed, F32), vmem(packed, F32), vmem(packed, BF16), vmem(packed, BF16),
        vmem(packed, F32), vmem(packed, F32), vmem(packed, BF16), vmem(packed, BF16),
        vmem((4, rows_o, depth), BF16), vmem((2, rows_o, depth), BF16),
        vmem((rows_o, depth), BF16), vmem((rows_o, depth), BF16),
        vmem((4, rows_v, width), BF16), vmem((2, rows_v, width), BF16),
        vmem((rows_v, width), BF16), vmem((rows_v, width), BF16),
        pltpu.SemaphoreType.DMA((8,)),
        pltpu.SemaphoreType.DMA((24,)),
        pltpu.SemaphoreType.DMA((24,)),
        pltpu.SemaphoreType.DMA((2, reps)),
        pltpu.SemaphoreType.DMA((2, reps)),
        pltpu.SemaphoreType.DMA((2, reps)),
        pltpu.SemaphoreType.DMA((2, reps)),
    ]
    outs = pl.pallas_call(
        functools.partial(kernel, reps, row_parts),
        out_shape=(
            jax.ShapeDtypeStruct((rows_v, width), BF16),
            jax.ShapeDtypeStruct((rows_o, depth), BF16),
        ),
        in_specs=[pl.BlockSpec(memory_space=pl.ANY)] * 8
        + [pl.BlockSpec(memory_space=pltpu.SMEM)] * 2,
        out_specs=(pl.BlockSpec(memory_space=vmem), pl.BlockSpec(memory_space=vmem)),
        scratch_shapes=scratch,
        compiler_params=pltpu.CompilerParams(
            collective_id=0, has_side_effects=True, vmem_limit_bytes=67043328
        ),
        name="gossip_step",
    )(*arrays, step_counts, partner)
    whole = pl.BlockSpec(memory_space=pl.ANY)
    outs = pl.pallas_call(
        hand_over,
        out_shape=tuple(jax.ShapeDtypeStruct(out.shape, BF16) for out in outs),
        in_specs=[whole] * 2,
        out_specs=(whole, whole),
        scratch_shapes=[vmem(out.shape, BF16) for out in outs]
        + [pltpu.SemaphoreType.DMA((2, 2 * CHUNKS))],
        name="hand_over",
    )(*outs)
    return outs[0][None], outs[1][None]


def solution(mesh):
    placed = (P("rep", "seq", None),) * 8 + (P(), P())
    return jax.shard_map(
        on_device,
        mesh=mesh,
        in_specs=placed,
        out_specs=(P("rep", "seq", None), P("rep", "seq", None)),
        check_vma=False,
    )
```

```python
import functools

import jax
import jax.numpy as jnp
from jax import lax
from jax.experimental import pallas as pl
from jax.experimental.pallas import tpu as pltpu
from jax.sharding import PartitionSpec as P

HEAD = 64
PAIR = 2 * HEAD
learning_rate = 0.25
norm_eps = 1e-06
F32 = jnp.float32
BF16 = jnp.bfloat16
TN = (((0,), (0,)), ((), ()))
NT = (((1,), (1,)), ((), ()))
CHUNKS = 2


def dot(a, b, dims=(((1,), (0,)), ((), ()))):
    return lax.dot_general(a, b, dims, preferred_element_type=F32)


def kernel(
    reps, row_parts,
    x_hbm, q_hbm, k_hbm, c_hbm, wv_hbm, wo_hbm, sv_hbm, so_hbm, counts, partner,
    nv_ref, no_ref,
    x, q, k, c, wv, wo, scores, acc, values, inv, normed, upstream, d_attn,
    spread_v, spread_o, pick_v, pick_o, mate_v, mate_o,
    state_own, state_sib, state_chip, state_far,
    later_own, later_sib, later_chip, later_far,
    part_o, sib_o, sum_o, far_o, part_v, sib_v, sum_v, far_v,
    load_sem, send_sem, recv_sem, spread_send, spread_recv, mate_send, mate_recv,
):
    rep = lax.axis_index("rep")
    me = lax.axis_index("seq")
    core = lax.rem(me, 2)
    chip = me // 2
    sib = chip * 2 + 1 - core
    far = (1 - chip) * 2 + core
    diag = (1 - chip) * 2 + 1 - core
    positions, depth = x.shape
    width = q.shape[1]
    half = positions // 2
    pairs = width // PAIR
    scale_value = depth ** (-0.5)
    scale_output = width ** (-0.5)
    used = [0]

    def remote(src, dst, target):
        index = used[0]
        used[0] += 1
        return pltpu.make_async_remote_copy(
            src_ref=src, dst_ref=dst, send_sem=send_sem.at[index], recv_sem=recv_sem.at[index],
            device_id={"seq": target}, device_id_type=pl.DeviceIdType.MESH,
        )

    barrier = pltpu.get_barrier_semaphore()
    for target in (sib, far):
        pl.semaphore_signal(
            barrier, inc=1, device_id={"seq": target}, device_id_type=pl.DeviceIdType.MESH
        )

    @pl.loop(1, reps)
    def _(step):
        pl.semaphore_signal(
            barrier, inc=1, device_id={"rep": lax.rem(rep + step, reps)},
            device_id_type=pl.DeviceIdType.MESH,
        )

    loads = [
        pltpu.make_async_copy(src, dst, load_sem.at[index])
        for index, (src, dst) in enumerate(
            ((q_hbm, q), (k_hbm, k), (wv_hbm, wv.at[me]), (x_hbm, x), (wo_hbm, wo.at[me]), (c_hbm, c))
        )
    ]
    for copy in loads:
        copy.start()
    pl.semaphore_wait(barrier, reps + 1)

    def split(rows):
        return [pl.ds(i * (rows // CHUNKS), rows // CHUNKS) for i in range(CHUNKS)]

    rows_v, rows_o = split(wv.shape[1]), split(wo.shape[1])
    far_wv = [remote(wv_hbm.at[r], wv.at[me, r], far) for r in rows_v]
    sib_wv = remote(wv_hbm, wv.at[me], sib)
    far_wo = [remote(wo_hbm.at[r], wo.at[me, r], far) for r in rows_o]
    sib_wo = remote(wo_hbm, wo.at[me], sib)
    pass_wv = [remote(wv.at[far, r], wv.at[far, r], sib) for r in rows_v]
    pass_wo = [remote(wo.at[far, r], wo.at[far, r], sib) for r in rows_o]
    for copy in far_wv:
        copy.start()
    sib_wv.start()
    far_wo[0].start()
    sib_wo.start()

    col_parts = reps // row_parts
    high_v, wide_v = spread_v.shape[1:]
    high_o, wide_o = spread_o.shape[1:]

    def place(index, high, wide):
        row = pl.multiple_of((index // col_parts) * high, high)
        column = pl.multiple_of(lax.rem(index, col_parts) * wide, wide)
        return pl.ds(row, high), pl.ds(column, wide)

    def piece(ref, index, high, wide):
        rows, columns = place(index, high, wide)
        return ref.at[rows, columns]

    sources = (sv_hbm, so_hbm)
    spreads = (spread_v, spread_o)
    picks = (pick_v, pick_o)
    mates = (mate_v, mate_o)
    extents = ((high_v, wide_v), (high_o, wide_o))

    side = reps // 2
    high, low = rep // side, lax.rem(rep, side)

    def exchange(step, kind, which):
        near = step // side
        group = high * near + (1 - high) * (1 - near)
        hop = step - near * (side - 1)
        target = group * side + lax.rem(low // 2 + hop // 2, side // 2) * 2 + lax.rem(low + hop, 2)
        if which == 0:
            src, dst = piece(sources[kind], target, *extents[kind]), spreads[kind]
            sems = (spread_send, spread_recv)
        else:
            src, dst = picks[kind].at[target], mates[kind]
            sems = (mate_send, mate_recv)
        return pltpu.make_async_remote_copy(
            src_ref=src, dst_ref=dst.at[rep], send_sem=sems[0].at[kind, step],
            recv_sem=sems[1].at[kind, step], device_id={"rep": target},
            device_id_type=pl.DeviceIdType.MESH,
        )

    def run_exchange(kind, which, act):
        @pl.loop(0, reps - 1)
        def _(step):
            act(exchange(step, kind, which))

    run_exchange(0, 0, lambda copy: copy.start())
    own_pieces = [
        pltpu.make_async_copy(piece(sv_hbm, rep, high_v, wide_v), spread_v.at[rep], load_sem.at[6]),
        pltpu.make_async_copy(piece(so_hbm, rep, high_o, wide_o), spread_o.at[rep], load_sem.at[7]),
    ]
    for copy in own_pieces:
        copy.start()

    mate = partner[rep]

    def pick(kind):
        own_pieces[kind].wait()
        run_exchange(kind, 0, lambda copy: copy.wait())

        @pl.loop(0, reps)
        def _(r):
            picks[kind][r] = spreads[kind][partner[r]]

        run_exchange(kind, 1, lambda copy: copy.start())
        mates[kind][rep] = spreads[kind][mate]

    def lanes(p):
        return pl.ds(pl.multiple_of(p * PAIR, PAIR), PAIR)

    def first_lanes(rows):
        return lax.broadcasted_iota(jnp.int32, (rows, PAIR), 1) < HEAD

    def diagonal():
        row = lax.broadcasted_iota(jnp.int32, (PAIR, PAIR), 0) < HEAD
        column = lax.broadcasted_iota(jnp.int32, (PAIR, PAIR), 1) < HEAD
        return row == column

    loads[0].wait()
    loads[1].wait()

    @pl.loop(0, pairs)
    def _(p):
        keys = k[:, lanes(p)]
        queries = q[:, lanes(p)]
        first = first_lanes(positions)
        zero = jnp.zeros_like(queries)
        causal = lax.broadcasted_iota(jnp.int32, (half, half), 0) >= lax.broadcasted_iota(
            jnp.int32, (half, half), 1
        )
        for h in range(2):
            mine = jnp.where(first, queries, zero) if h == 0 else jnp.where(first, zero, queries)
            head = p * 2 + h
            low = dot(mine[half:], keys[:half], NT)
            scores[head, half:, :half] = low.astype(BF16)
            for b in range(2):
                block = slice(b * half, (b + 1) * half)
                square = dot(mine[block], keys[block], NT)
                scores[head, block, block] = jnp.where(causal, square, 0.0).astype(BF16)

    tile = 256

    def add_values(block, begin):
        columns = pl.ds(pl.multiple_of(block * wv.shape[1], wv.shape[1]), wv.shape[1])

        @pl.loop(0, width // tile)
        def _(n):
            out = pl.ds(pl.multiple_of(n * tile, tile), tile)
            term = dot(x[:, columns], wv[block, :, out])
            acc[:, out] = term if begin else acc[:, out] + term

    def add_upstream(block):
        rows = wo.shape[1]
        upstream[:, pl.ds(pl.multiple_of(block * rows, rows), rows)] = (
            dot(c[...], wo[block], NT) * scale_output
        )

    loads[2].wait()
    loads[3].wait()
    add_values(me, True)
    sib_wv.wait()
    add_values(sib, False)
    loads[4].wait()
    loads[5].wait()
    add_upstream(me)
    sib_wo.wait()
    add_upstream(sib)
    for arrive, forward in zip(far_wv, pass_wv):
        arrive.wait()
        forward.start()
    run_exchange(1, 0, lambda copy: copy.start())
    add_values(far, False)
    for forward in pass_wv:
        forward.wait()
    add_values(diag, False)

    @pl.loop(0, width // tile)
    def _(n):
        out = pl.ds(pl.multiple_of(n * tile, tile), tile)
        values[:, out] = (acc[:, out] * scale_value).astype(BF16)

    def states(left, right, own):
        @pl.loop(0, pairs // 2)
        def _(j):
            same = diagonal()
            terms = [
                dot(left[:, lanes(2 * j + i)], right[:, lanes(2 * j + i)], TN) for i in range(2)
            ]
            own[j] = jnp.where(same, terms[0], pltpu.roll(jnp.where(same, terms[1], 0.0), HEAD, 1))

    def unpack(packed, i):
        same = diagonal()
        if i == 0:
            return jnp.where(same, packed, 0.0)
        return pltpu.roll(jnp.where(same, 0.0, packed), HEAD, 1)

    def chip_share(total, landed, sender):
        count = total.shape[0] // 2
        mine = pl.ds(core * count, count)
        cross = remote(total.at[mine], landed.at[mine], far)
        across = remote(landed.at[mine], landed.at[mine], sib)

        def start():
            @pl.when(chip == sender)
            def _():
                landed[...] = jnp.zeros_like(landed)
                cross.start()

        def wait():
            @pl.when(chip == sender)
            def _():
                cross.wait_send()

            @pl.when(chip != sender)
            def _():
                cross.wait_recv()
                across.start()
                across.wait()

        return start, wait

    states(k, values, state_own)
    to_sib = remote(state_own, state_sib, sib)
    to_far = chip_share(state_chip, state_far, 0)
    to_sib.start()
    to_sib.wait()
    state_chip[...] = (state_own[...] + state_sib[...]).astype(BF16)
    to_far[0]()
    far_wo[1].start()

    @pl.loop(0, pairs // 2)
    def _(p2):
        for i in range(2):
            p = p2 * 2 + i
            right = values[:, lanes(p)]
            first = first_lanes(half)
            for b in range(2):
                rows = slice(b * half, (b + 1) * half)
                both = [dot(scores[p * 2 + h, rows, : (b + 1) * half], right[: (b + 1) * half]) for h in range(2)]
                acc[rows, lanes(p)] = jnp.where(first, both[0], both[1])

    to_far[1]()
    after_core = (core == 1).astype(F32)
    after_chip = (chip == 1).astype(F32)

    def head_mean(array, first):
        low = jnp.sum(jnp.where(first, array, 0.0), axis=1, keepdims=True)
        high = jnp.sum(jnp.where(first, 0.0, array), axis=1, keepdims=True)
        return jnp.where(first, low, high) * (1.0 / HEAD)

    @pl.loop(0, pairs // 2)
    def _(j):
        packed = after_core * state_sib[j] + after_chip * state_far[j].astype(F32)
        first = first_lanes(positions)
        for i in range(2):
            span = lanes(2 * j + i)
            prior = unpack(packed, i).astype(BF16)
            attn = acc[:, span] + dot(q[:, span], prior)
            inverse = lax.rsqrt(head_mean(attn * attn, first) + norm_eps)
            unit = attn * inverse
            acc[:, span] = unit
            inv[:, span] = inverse
            normed[:, span] = unit.astype(BF16)

    def tile_o(slot, dest):
        rows = part_o.shape[1]
        left = normed[:, pl.ds(pl.multiple_of(dest * rows, rows), rows)]
        step = depth // 4

        @pl.loop(0, 4)
        def _(n):
            out = pl.ds(pl.multiple_of(n * step, step), step)
            part_o[slot, :, out] = (dot(left, c[:, out], TN) * scale_output).astype(BF16)

    def tile_v(slot, dest):
        rows = part_v.shape[1]

        @pl.loop(0, width // tile)
        def _(n):
            out = pl.ds(pl.multiple_of(n * tile, tile), tile)
            left = x[:, pl.ds(pl.multiple_of(dest * rows, rows), rows)]
            part_v[slot, :, out] = (dot(left, values[:, out], TN) * scale_value).astype(BF16)

    def scatter(make_tile, part, from_sib, total, landed):
        rows = split(part.shape[1])
        pair_far = remote(part.at[0], from_sib.at[0], sib)
        pair_near = remote(part.at[2], from_sib.at[1], sib)
        cross = [remote(total.at[r], landed.at[r], far) for r in rows]
        make_tile(0, diag)
        pair_far.start()
        make_tile(1, far)
        pair_far.wait()
        total[...] = (part[1].astype(F32) + from_sib[0].astype(F32)).astype(BF16)
        return pair_near, cross

    near_o, cross_o = scatter(tile_o, part_o, sib_o, sum_o, far_o)
    cross_o[0].start()
    pick(0)
    for arrive, forward in zip(far_wo, pass_wo):
        arrive.wait()
        forward.start()
    add_upstream(far)
    for forward in pass_wo:
        forward.wait()
    add_upstream(diag)

    @pl.loop(0, pairs)
    def _(p):
        span = lanes(p)
        first = first_lanes(positions)
        up = upstream[:, span]
        unit = acc[:, span]
        d_attn[:, span] = (inv[:, span] * (up - unit * head_mean(unit * up, first))).astype(BF16)

    states(q, d_attn, later_own)
    later_to_sib = remote(later_own, later_sib, sib)
    later_to_far = chip_share(later_chip, later_far, 1)
    later_to_sib.start()
    later_to_sib.wait()
    later_chip[...] = (later_own[...] + later_sib[...]).astype(BF16)
    later_to_far[0]()
    cross_o[1].start()
    pick(1)

    @pl.loop(0, pairs)
    def _(p):
        right = d_attn[:, lanes(p)]
        first = first_lanes(half)
        for b in range(2):
            rows = slice(b * half, (b + 1) * half)
            both = [dot(scores[p * 2 + h, b * half :, rows], right[b * half :], TN) for h in range(2)]
            acc[rows, lanes(p)] = jnp.where(first, both[0], both[1])

    later_to_far[1]()
    before_core = (core == 0).astype(F32)
    before_chip = (chip == 0).astype(F32)

    @pl.loop(0, pairs // 2)
    def _(j):
        packed = before_core * later_sib[j] + before_chip * later_far[j].astype(F32)
        for i in range(2):
            span = lanes(2 * j + i)
            later = unpack(packed, i).astype(BF16)
            values[:, span] = (acc[:, span] + dot(k[:, span], later)).astype(BF16)

    near_v, cross_v = scatter(tile_v, part_v, sib_v, sum_v, far_v)
    for copy in cross_v:
        copy.start()
    tile_o(2, sib)
    near_o.start()
    tile_o(3, me)
    tile_v(2, sib)
    near_v.start()
    tile_v(3, me)

    own_count = counts[rep].astype(F32)
    mate_count = counts[mate].astype(F32)
    share = jnp.full((1, 128), mate_count, F32) / jnp.full((1, 128), own_count + mate_count, F32)
    mix = share[0:1, 0:1]

    run_exchange(0, 1, lambda copy: copy.wait())
    near_v.wait()

    def finish(out, weight, theirs, part, from_sib, landed, high, wide, begin, end):
        @pl.loop(begin, end)
        def _(index):
            at = place(index, high, wide)
            grad = part[(3, *at)].astype(F32) + from_sib[(1, *at)].astype(F32) + landed[at].astype(F32)
            mixed = (1.0 - mix) * weight[(me, *at)].astype(F32) + mix * theirs[index].astype(F32)
            out[at] = (mixed - learning_rate * grad).astype(BF16)

    for i, copy in enumerate(cross_v):
        copy.wait()
        finish(
            nv_ref, wv, mates[0], part_v, sib_v, far_v, high_v, wide_v,
            i * reps // CHUNKS, (i + 1) * reps // CHUNKS,
        )
    near_o.wait()
    for copy in cross_o:
        copy.wait()
    run_exchange(1, 1, lambda copy: copy.wait())
    finish(no_ref, wo, mates[1], part_o, sib_o, far_o, high_o, wide_o, 0, reps)


def hand_over(*refs):
    sources, results, sems = refs[:2], refs[2:4], refs[4]
    copies = []
    for kind in range(2):
        step = sources[kind].shape[0] // CHUNKS
        for i in range(CHUNKS):
            rows = pl.ds(i * step, step)
            copies.append(pltpu.make_async_copy(sources[kind].at[rows], results[kind].at[rows], sems.at[kind * CHUNKS + i]))
    for copy in copies:
        copy.start()
    for copy in copies:
        copy.wait()


def on_device(
    inputs, query, key_feat, cotangent, value_weight, output_weight, stale_value, stale_output,
    step_counts, partner,
):
    arrays = [
        a[0] for a in (inputs, query, key_feat, cotangent, value_weight, output_weight, stale_value, stale_output)
    ]
    reps = lax.axis_size("rep")
    seqs = lax.axis_size("seq")
    positions, depth = arrays[0].shape
    width = arrays[1].shape[1]
    rows_v, rows_o = arrays[4].shape[0], arrays[5].shape[0]
    row_parts = min(reps, 8)
    col_parts = reps // row_parts
    piece_v = (reps, rows_v // row_parts, width // col_parts)
    piece_o = (reps, rows_o // row_parts, depth // col_parts)
    packed = (width // PAIR // 2, PAIR, PAIR)
    vmem = pltpu.VMEM
    scratch = [
        vmem((positions, depth), BF16),
        vmem((positions, width), BF16),
        vmem((positions, width), BF16),
        vmem((positions, depth), BF16),
        vmem((seqs, rows_v, width), BF16),
        vmem((seqs, rows_o, depth), BF16),
        vmem((width // HEAD, positions, positions), BF16),
        vmem((positions, width), F32),
        vmem((positions, width), BF16),
        vmem((positions, width), F32),
        vmem((positions, width), BF16),
        vmem((positions, width), F32),
        vmem((positions, width), BF16),
        vmem(piece_v, BF16), vmem(piece_o, BF16),
        vmem(piece_v, BF16), vmem(piece_o, BF16),
        vmem(piece_v, BF16), vmem(piece_o, BF16),
        vmem(packed, F32), vmem(packed, F32), vmem(packed, BF16), vmem(packed, BF16),
        vmem(packed, F32), vmem(packed, F32), vmem(packed, BF16), vmem(packed, BF16),
        vmem((4, rows_o, depth), BF16), vmem((2, rows_o, depth), BF16),
        vmem((rows_o, depth), BF16), vmem((rows_o, depth), BF16),
        vmem((4, rows_v, width), BF16), vmem((2, rows_v, width), BF16),
        vmem((rows_v, width), BF16), vmem((rows_v, width), BF16),
        pltpu.SemaphoreType.DMA((8,)),
        pltpu.SemaphoreType.DMA((24,)),
        pltpu.SemaphoreType.DMA((24,)),
        pltpu.SemaphoreType.DMA((2, reps)),
        pltpu.SemaphoreType.DMA((2, reps)),
        pltpu.SemaphoreType.DMA((2, reps)),
        pltpu.SemaphoreType.DMA((2, reps)),
    ]
    outs = pl.pallas_call(
        functools.partial(kernel, reps, row_parts),
        out_shape=(vmem((rows_v, width), BF16), vmem((rows_o, depth), BF16)),
        in_specs=[pl.BlockSpec(memory_space=pl.ANY)] * 8
        + [pl.BlockSpec(memory_space=pltpu.SMEM)] * 2,
        out_specs=(pl.BlockSpec(memory_space=vmem), pl.BlockSpec(memory_space=vmem)),
        scratch_shapes=scratch,
        compiler_params=pltpu.CompilerParams(
            collective_id=0, has_side_effects=True, vmem_limit_bytes=64749568
        ),
        name="gossip_step",
    )(*arrays, step_counts, partner)
    whole = pl.BlockSpec(memory_space=pl.ANY)
    outs = [pltpu.with_memory_space_constraint(out, pltpu.VMEM) for out in outs]
    outs = pl.pallas_call(
        hand_over,
        out_shape=tuple(jax.ShapeDtypeStruct(out.shape, BF16) for out in outs),
        in_specs=[pl.BlockSpec(memory_space=vmem)] * 2,
        out_specs=(whole, whole),
        scratch_shapes=[pltpu.SemaphoreType.DMA((2 * CHUNKS,))],
        compiler_params=pltpu.CompilerParams(vmem_limit_bytes=2**20),
        name="hand_over",
    )(*outs)
    return outs[0][None], outs[1][None]


def solution(mesh):
    placed = (P("rep", "seq", None),) * 8 + (P(), P())
    return jax.shard_map(
        on_device,
        mesh=mesh,
        in_specs=placed,
        out_specs=(P("rep", "seq", None), P("rep", "seq", None)),
        check_vma=False,
    )
```

```python
import functools

import jax
import jax.numpy as jnp
from jax import lax
from jax.experimental import pallas as pl
from jax.experimental.pallas import tpu as pltpu
from jax.sharding import PartitionSpec as P

HEAD = 64
PAIR = 2 * HEAD
learning_rate = 0.25
norm_eps = 1e-06
F32 = jnp.float32
BF16 = jnp.bfloat16
TN = (((0,), (0,)), ((), ()))
NT = (((1,), (1,)), ((), ()))
CHUNKS = 2


def dot(a, b, dims=(((1,), (0,)), ((), ()))):
    return lax.dot_general(a, b, dims, preferred_element_type=F32)


def kernel(
    reps, row_parts,
    x_hbm, q_hbm, k_hbm, c_hbm, wv_hbm, wo_hbm, sv_hbm, so_hbm, counts, partner,
    nv_ref, no_ref,
    x, q, k, c, wv, wo, scores, acc, values, inv, normed, upstream, d_attn,
    spread_v, spread_o, pick_v, pick_o, mate_v, mate_o,
    state_own, state_sib, state_chip, state_far,
    later_own, later_sib, later_chip, later_far,
    part_o, sib_o, sum_o, far_o, part_v, sib_v, sum_v, far_v,
    load_sem, send_sem, recv_sem, spread_send, spread_recv, mate_send, mate_recv, ready,
):
    rep = lax.axis_index("rep")
    me = lax.axis_index("seq")
    core = lax.rem(me, 2)
    chip = me // 2
    sib = chip * 2 + 1 - core
    far = (1 - chip) * 2 + core
    diag = (1 - chip) * 2 + 1 - core
    positions, depth = x.shape
    width = q.shape[1]
    half = positions // 2
    pairs = width // PAIR
    scale_value = depth ** (-0.5)
    scale_output = width ** (-0.5)
    used = [0]

    def remote(src, dst, target):
        index = used[0]
        used[0] += 1
        return pltpu.make_async_remote_copy(
            src_ref=src, dst_ref=dst, send_sem=send_sem.at[index], recv_sem=recv_sem.at[index],
            device_id={"seq": target}, device_id_type=pl.DeviceIdType.MESH,
        )

    barrier = pltpu.get_barrier_semaphore()

    def tell(semaphore, target):
        pl.semaphore_signal(semaphore, inc=1, device_id=target, device_id_type=pl.DeviceIdType.MESH)

    def tell_reps(semaphore):
        @pl.loop(1, reps)
        def _(step):
            tell(semaphore, {"rep": lax.rem(rep + step, reps)})

    tell(barrier, {"seq": far})

    @pl.when(core == 0)
    def _():
        tell(barrier, {"seq": sib})

    @pl.when(core == 1)
    def _():
        tell_reps(barrier)

    loads = [
        pltpu.make_async_copy(src, dst, load_sem.at[index])
        for index, (src, dst) in enumerate(
            ((q_hbm, q), (k_hbm, k), (wv_hbm, wv.at[me]), (x_hbm, x), (wo_hbm, wo.at[me]), (c_hbm, c))
        )
    ]
    for copy in loads:
        copy.start()
    def split(rows, count=CHUNKS):
        return [pl.ds(i * (rows // count), rows // count) for i in range(count)]

    rows_v, rows_o = split(wv.shape[1]), split(wo.shape[1])
    far_wv = [remote(wv_hbm.at[r], wv.at[me, r], far) for r in rows_v]
    sib_wv = remote(wv_hbm, wv.at[me], sib)
    far_wo = [remote(wo_hbm.at[r], wo.at[me, r], far) for r in rows_o]
    sib_wo = remote(wo_hbm, wo.at[me], sib)
    pass_wv = [remote(wv.at[far, r], wv.at[far, r], sib) for r in rows_v]
    pass_wo = [remote(wo.at[far, r], wo.at[far, r], sib) for r in rows_o]
    early = far_wv + far_wo[:1]

    @pl.when(core == 0)
    def _():
        pl.semaphore_wait(barrier, 1)
        for copy in early:
            copy.start()
        pl.semaphore_wait(ready.at[0], 1)

    @pl.when(core == 1)
    def _():
        pl.semaphore_wait(barrier, reps + 1)
        for copy in early:
            copy.start()
        tell(ready.at[0], {"seq": sib})
        tell_reps(ready.at[1])

    sib_wv.start()
    sib_wo.start()

    col_parts = reps // row_parts
    high_v, wide_v = spread_v.shape[1:]
    high_o, wide_o = spread_o.shape[1:]

    def place(index, high, wide):
        row = pl.multiple_of((index // col_parts) * high, high)
        column = pl.multiple_of(lax.rem(index, col_parts) * wide, wide)
        return pl.ds(row, high), pl.ds(column, wide)

    def piece(ref, index, high, wide):
        rows, columns = place(index, high, wide)
        return ref.at[rows, columns]

    sources = (sv_hbm, so_hbm)
    spreads = (spread_v, spread_o)
    picks = (pick_v, pick_o)
    mates = (mate_v, mate_o)
    extents = ((high_v, wide_v), (high_o, wide_o))

    side = reps // 2
    high, low = rep // side, lax.rem(rep, side)

    def exchange(step, kind, which):
        near = step // side
        group = high * near + (1 - high) * (1 - near)
        hop = step - near * (side - 1)
        target = group * side + lax.rem(low // 2 + hop // 2, side // 2) * 2 + lax.rem(low + hop, 2)
        if which == 0:
            src, dst = piece(sources[kind], target, *extents[kind]), spreads[kind]
            sems = (spread_send, spread_recv)
        else:
            src, dst = picks[kind].at[target], mates[kind]
            sems = (mate_send, mate_recv)
        return pltpu.make_async_remote_copy(
            src_ref=src, dst_ref=dst.at[rep], send_sem=sems[0].at[kind, step],
            recv_sem=sems[1].at[kind, step], device_id={"rep": target},
            device_id_type=pl.DeviceIdType.MESH,
        )

    def sender(step):
        near = step // side
        group = high * near + (1 - high) * (1 - near)
        hop = step - near * (side - 1)
        pair = lax.rem(low // 2 + side // 2 - hop // 2, side // 2)
        return group * side + pair * 2 + lax.rem(low + hop, 2)

    def run_exchange(kind, which, act):
        @pl.loop(0, reps - 1)
        def _(step):
            act(exchange(step, kind, which))

    @pl.when(core == 0)
    def _():
        pl.semaphore_wait(ready.at[2], 1)

    run_exchange(0, 0, lambda copy: copy.start())

    @pl.when(core == 1)
    def _():
        pl.semaphore_wait(ready.at[1], reps - 1)
        tell(ready.at[2], {"seq": sib})

    own_pieces = [
        pltpu.make_async_copy(piece(sv_hbm, rep, high_v, wide_v), spread_v.at[rep], load_sem.at[6]),
        pltpu.make_async_copy(piece(so_hbm, rep, high_o, wide_o), spread_o.at[rep], load_sem.at[7]),
    ]
    for copy in own_pieces:
        copy.start()

    mate = partner[rep]

    def pick(kind):
        own_pieces[kind].wait()
        run_exchange(kind, 0, lambda copy: copy.wait())

        @pl.loop(0, reps)
        def _(r):
            picks[kind][r] = spreads[kind][partner[r]]

        run_exchange(kind, 1, lambda copy: copy.start())
        mates[kind][rep] = spreads[kind][mate]

    def lanes(p):
        return pl.ds(pl.multiple_of(p * PAIR, PAIR), PAIR)

    def first_lanes(rows):
        return lax.broadcasted_iota(jnp.int32, (rows, PAIR), 1) < HEAD

    def diagonal():
        row = lax.broadcasted_iota(jnp.int32, (PAIR, PAIR), 0) < HEAD
        column = lax.broadcasted_iota(jnp.int32, (PAIR, PAIR), 1) < HEAD
        return row == column

    loads[0].wait()
    loads[1].wait()

    @pl.loop(0, pairs)
    def _(p):
        keys = k[:, lanes(p)]
        queries = q[:, lanes(p)]
        first = first_lanes(positions)
        zero = jnp.zeros_like(queries)
        causal = lax.broadcasted_iota(jnp.int32, (half, half), 0) >= lax.broadcasted_iota(
            jnp.int32, (half, half), 1
        )
        for h in range(2):
            mine = jnp.where(first, queries, zero) if h == 0 else jnp.where(first, zero, queries)
            head = p * 2 + h
            low = dot(mine[half:], keys[:half], NT)
            scores[head, half:, :half] = low.astype(BF16)
            for b in range(2):
                block = slice(b * half, (b + 1) * half)
                square = dot(mine[block], keys[block], NT)
                scores[head, block, block] = jnp.where(causal, square, 0.0).astype(BF16)

    tile = 256

    def add_values(block, begin):
        columns = pl.ds(pl.multiple_of(block * wv.shape[1], wv.shape[1]), wv.shape[1])

        @pl.loop(0, width // tile)
        def _(n):
            out = pl.ds(pl.multiple_of(n * tile, tile), tile)
            term = dot(x[:, columns], wv[block, :, out])
            acc[:, out] = term if begin else acc[:, out] + term

    def add_upstream(block):
        rows = wo.shape[1]
        upstream[:, pl.ds(pl.multiple_of(block * rows, rows), rows)] = (
            dot(c[...], wo[block], NT) * scale_output
        )

    loads[2].wait()
    loads[3].wait()
    add_values(me, True)
    sib_wv.wait()
    add_values(sib, False)
    loads[4].wait()
    loads[5].wait()
    add_upstream(me)
    sib_wo.wait()
    add_upstream(sib)
    for arrive, forward in zip(far_wv, pass_wv):
        arrive.wait()
        forward.start()
    run_exchange(1, 0, lambda copy: copy.start())
    add_values(far, False)
    for forward in pass_wv:
        forward.wait()
    add_values(diag, False)

    @pl.loop(0, width // tile)
    def _(n):
        out = pl.ds(pl.multiple_of(n * tile, tile), tile)
        values[:, out] = (acc[:, out] * scale_value).astype(BF16)

    def states(left, right, own):
        @pl.loop(0, pairs // 2)
        def _(j):
            same = diagonal()
            terms = [
                dot(left[:, lanes(2 * j + i)], right[:, lanes(2 * j + i)], TN) for i in range(2)
            ]
            own[j] = jnp.where(same, terms[0], pltpu.roll(jnp.where(same, terms[1], 0.0), HEAD, 1))

    def unpack(packed, i):
        same = diagonal()
        if i == 0:
            return jnp.where(same, packed, 0.0)
        return pltpu.roll(jnp.where(same, 0.0, packed), HEAD, 1)

    def chip_share(total, landed, sender):
        count = total.shape[0] // 2
        mine = pl.ds(core * count, count)
        cross = remote(total.at[mine], landed.at[mine], far)
        across = remote(landed.at[mine], landed.at[mine], sib)

        def start():
            @pl.when(chip == sender)
            def _():
                landed[...] = jnp.zeros_like(landed)
                cross.start()

        def wait():
            @pl.when(chip == sender)
            def _():
                cross.wait_send()

            @pl.when(chip != sender)
            def _():
                cross.wait_recv()
                across.start()
                across.wait()

        return start, wait

    states(k, values, state_own)
    to_sib = remote(state_own, state_sib, sib)
    to_far = chip_share(state_chip, state_far, 0)
    to_sib.start()
    to_sib.wait()
    state_chip[...] = (state_own[...] + state_sib[...]).astype(BF16)
    to_far[0]()
    far_wo[1].start()

    @pl.loop(0, pairs // 2)
    def _(p2):
        for i in range(2):
            p = p2 * 2 + i
            right = values[:, lanes(p)]
            first = first_lanes(half)
            for b in range(2):
                rows = slice(b * half, (b + 1) * half)
                both = [dot(scores[p * 2 + h, rows, : (b + 1) * half], right[: (b + 1) * half]) for h in range(2)]
                acc[rows, lanes(p)] = jnp.where(first, both[0], both[1])

    to_far[1]()
    after_core = (core == 1).astype(F32)
    after_chip = (chip == 1).astype(F32)

    def head_mean(array, first):
        low = jnp.sum(jnp.where(first, array, 0.0), axis=1, keepdims=True)
        high = jnp.sum(jnp.where(first, 0.0, array), axis=1, keepdims=True)
        return jnp.where(first, low, high) * (1.0 / HEAD)

    @pl.loop(0, pairs // 2)
    def _(j):
        packed = after_core * state_sib[j] + after_chip * state_far[j].astype(F32)
        first = first_lanes(positions)
        for i in range(2):
            span = lanes(2 * j + i)
            prior = unpack(packed, i).astype(BF16)
            attn = acc[:, span] + dot(q[:, span], prior)
            inverse = lax.rsqrt(head_mean(attn * attn, first) + norm_eps)
            unit = attn * inverse
            acc[:, span] = unit
            inv[:, span] = inverse
            normed[:, span] = unit.astype(BF16)

    def tile_o(slot, dest):
        rows = part_o.shape[1]
        left = normed[:, pl.ds(pl.multiple_of(dest * rows, rows), rows)]
        step = depth // 4

        @pl.loop(0, 4)
        def _(n):
            out = pl.ds(pl.multiple_of(n * step, step), step)
            part_o[slot, :, out] = (dot(left, c[:, out], TN) * scale_output).astype(BF16)

    def tile_v(slot, dest):
        rows = part_v.shape[1]

        @pl.loop(0, width // tile)
        def _(n):
            out = pl.ds(pl.multiple_of(n * tile, tile), tile)
            left = x[:, pl.ds(pl.multiple_of(dest * rows, rows), rows)]
            part_v[slot, :, out] = (dot(left, values[:, out], TN) * scale_value).astype(BF16)

    def scatter(make_tile, part, from_sib, total, landed, count):
        rows = split(part.shape[1], count)
        pair_far = remote(part.at[0], from_sib.at[0], sib)
        pair_near = remote(part.at[2], from_sib.at[1], sib)
        cross = [remote(total.at[r], landed.at[r], far) for r in rows]
        make_tile(0, diag)
        pair_far.start()
        make_tile(1, far)
        pair_far.wait()
        total[...] = (part[1].astype(F32) + from_sib[0].astype(F32)).astype(BF16)
        return pair_near, cross

    near_o, cross_o = scatter(tile_o, part_o, sib_o, sum_o, far_o, CHUNKS)
    cross_o[0].start()
    pick(0)
    for arrive, forward in zip(far_wo, pass_wo):
        arrive.wait()
        forward.start()
    add_upstream(far)
    for forward in pass_wo:
        forward.wait()
    add_upstream(diag)

    @pl.loop(0, pairs)
    def _(p):
        span = lanes(p)
        first = first_lanes(positions)
        up = upstream[:, span]
        unit = acc[:, span]
        d_attn[:, span] = (inv[:, span] * (up - unit * head_mean(unit * up, first))).astype(BF16)

    states(q, d_attn, later_own)
    later_to_sib = remote(later_own, later_sib, sib)
    later_to_far = chip_share(later_chip, later_far, 1)
    later_to_sib.start()
    later_to_sib.wait()
    later_chip[...] = (later_own[...] + later_sib[...]).astype(BF16)
    later_to_far[0]()
    cross_o[1].start()

    @pl.loop(0, pairs)
    def _(p):
        right = d_attn[:, lanes(p)]
        first = first_lanes(half)
        for b in range(2):
            rows = slice(b * half, (b + 1) * half)
            both = [dot(scores[p * 2 + h, b * half :, rows], right[b * half :], TN) for h in range(2)]
            acc[rows, lanes(p)] = jnp.where(first, both[0], both[1])

    pick(1)
    later_to_far[1]()
    before_core = (core == 0).astype(F32)
    before_chip = (chip == 0).astype(F32)

    @pl.loop(0, pairs // 2)
    def _(j):
        packed = before_core * later_sib[j] + before_chip * later_far[j].astype(F32)
        for i in range(2):
            span = lanes(2 * j + i)
            later = unpack(packed, i).astype(BF16)
            values[:, span] = (acc[:, span] + dot(k[:, span], later)).astype(BF16)

    near_v, cross_v = scatter(tile_v, part_v, sib_v, sum_v, far_v, 2 * CHUNKS)
    for copy in cross_v:
        copy.start()
    tile_o(2, sib)
    near_o.start()
    tile_o(3, me)
    tile_v(2, sib)
    near_v.start()
    tile_v(3, me)

    own_count = counts[rep].astype(F32)
    mate_count = counts[mate].astype(F32)
    share = jnp.full((1, 128), mate_count, F32) / jnp.full((1, 128), own_count + mate_count, F32)
    mix = share[0:1, 0:1]

    run_exchange(0, 1, lambda copy: copy.wait())
    near_v.wait()

    def finish(out, weight, theirs, part, from_sib, landed, high, wide, index):
        at = place(index, high, wide)
        grad = part[(3, *at)].astype(F32) + from_sib[(1, *at)].astype(F32) + landed[at].astype(F32)
        mixed = (1.0 - mix) * weight[(me, *at)].astype(F32) + mix * theirs[index].astype(F32)
        out[at] = (mixed - learning_rate * grad).astype(BF16)

    def finish_o(index):
        finish(no_ref, wo, mates[1], part_o, sib_o, far_o, high_o, wide_o, index)

    near_o.wait()
    for copy in cross_o:
        copy.wait()
    finish_o(rep)
    parts_v = len(cross_v)
    for i, copy in enumerate(cross_v):
        copy.wait()

        @pl.loop(i * reps // parts_v, (i + 1) * reps // parts_v)
        def _(index):
            finish(nv_ref, wv, mates[0], part_v, sib_v, far_v, high_v, wide_v, index)

    @pl.loop(0, reps - 1)
    def _(step):
        exchange(step, 1, 1).wait()
        finish_o(sender(step))


def hand_over(*refs):
    sources, results, sems = refs[:2], refs[2:4], refs[4]
    copies = []
    for kind in range(2):
        step = sources[kind].shape[0] // CHUNKS
        for i in range(CHUNKS):
            rows = pl.ds(i * step, step)
            copies.append(pltpu.make_async_copy(sources[kind].at[rows], results[kind].at[rows], sems.at[kind * CHUNKS + i]))
    for copy in copies:
        copy.start()
    for copy in copies:
        copy.wait()


def on_device(
    inputs, query, key_feat, cotangent, value_weight, output_weight, stale_value, stale_output,
    step_counts, partner,
):
    arrays = [
        a[0] for a in (inputs, query, key_feat, cotangent, value_weight, output_weight, stale_value, stale_output)
    ]
    reps = lax.axis_size("rep")
    seqs = lax.axis_size("seq")
    positions, depth = arrays[0].shape
    width = arrays[1].shape[1]
    rows_v, rows_o = arrays[4].shape[0], arrays[5].shape[0]
    row_parts = min(reps, 8)
    col_parts = reps // row_parts
    piece_v = (reps, rows_v // row_parts, width // col_parts)
    piece_o = (reps, rows_o // row_parts, depth // col_parts)
    packed = (width // PAIR // 2, PAIR, PAIR)
    vmem = pltpu.VMEM
    scratch = [
        vmem((positions, depth), BF16),
        vmem((positions, width), BF16),
        vmem((positions, width), BF16),
        vmem((positions, depth), BF16),
        vmem((seqs, rows_v, width), BF16),
        vmem((seqs, rows_o, depth), BF16),
        vmem((width // HEAD, positions, positions), BF16),
        vmem((positions, width), F32),
        vmem((positions, width), BF16),
        vmem((positions, width), F32),
        vmem((positions, width), BF16),
        vmem((positions, width), F32),
        vmem((positions, width), BF16),
        vmem(piece_v, BF16), vmem(piece_o, BF16),
        vmem(piece_v, BF16), vmem(piece_o, BF16),
        vmem(piece_v, BF16), vmem(piece_o, BF16),
        vmem(packed, F32), vmem(packed, F32), vmem(packed, BF16), vmem(packed, BF16),
        vmem(packed, F32), vmem(packed, F32), vmem(packed, BF16), vmem(packed, BF16),
        vmem((4, rows_o, depth), BF16), vmem((2, rows_o, depth), BF16),
        vmem((rows_o, depth), BF16), vmem((rows_o, depth), BF16),
        vmem((4, rows_v, width), BF16), vmem((2, rows_v, width), BF16),
        vmem((rows_v, width), BF16), vmem((rows_v, width), BF16),
        pltpu.SemaphoreType.DMA((8,)),
        pltpu.SemaphoreType.DMA((26,)),
        pltpu.SemaphoreType.DMA((26,)),
        pltpu.SemaphoreType.DMA((2, reps)),
        pltpu.SemaphoreType.DMA((2, reps)),
        pltpu.SemaphoreType.DMA((2, reps)),
        pltpu.SemaphoreType.DMA((2, reps)),
        pltpu.SemaphoreType.REGULAR((3,)),
    ]
    outs = pl.pallas_call(
        functools.partial(kernel, reps, row_parts),
        out_shape=(vmem((rows_v, width), BF16), vmem((rows_o, depth), BF16)),
        in_specs=[pl.BlockSpec(memory_space=pl.ANY)] * 8
        + [pl.BlockSpec(memory_space=pltpu.SMEM)] * 2,
        out_specs=(pl.BlockSpec(memory_space=vmem), pl.BlockSpec(memory_space=vmem)),
        scratch_shapes=scratch,
        compiler_params=pltpu.CompilerParams(
            collective_id=0, has_side_effects=True, vmem_limit_bytes=64749568
        ),
        name="gossip_step",
    )(*arrays, step_counts, partner)
    whole = pl.BlockSpec(memory_space=pl.ANY)
    outs = [pltpu.with_memory_space_constraint(out, pltpu.VMEM) for out in outs]
    outs = pl.pallas_call(
        hand_over,
        out_shape=tuple(jax.ShapeDtypeStruct(out.shape, BF16) for out in outs),
        in_specs=[pl.BlockSpec(memory_space=vmem)] * 2,
        out_specs=(whole, whole),
        scratch_shapes=[pltpu.SemaphoreType.DMA((2 * CHUNKS,))],
        compiler_params=pltpu.CompilerParams(vmem_limit_bytes=2**20),
        name="hand_over",
    )(*outs)
    return outs[0][None], outs[1][None]


def solution(mesh):
    placed = (P("rep", "seq", None),) * 8 + (P(), P())
    return jax.shard_map(
        on_device,
        mesh=mesh,
        in_specs=placed,
        out_specs=(P("rep", "seq", None), P("rep", "seq", None)),
        check_vma=False,
    )
```

```python
import functools

import jax
import jax.numpy as jnp
from jax import lax
from jax.experimental import pallas as pl
from jax.experimental.pallas import tpu as pltpu
from jax.sharding import PartitionSpec as P

HEAD = 64
PAIR = 2 * HEAD
learning_rate = 0.25
norm_eps = 1e-06
F32 = jnp.float32
BF16 = jnp.bfloat16
TN = (((0,), (0,)), ((), ()))
NT = (((1,), (1,)), ((), ()))
CHUNKS = 2


def dot(a, b, dims=(((1,), (0,)), ((), ()))):
    return lax.dot_general(a, b, dims, preferred_element_type=F32)


def kernel(
    reps, row_parts,
    x_hbm, q_hbm, k_hbm, c_hbm, wv_hbm, wo_hbm, sv_hbm, so_hbm, counts, partner,
    nv_ref, no_ref,
    x, q, k, c, wv, wo, scores, acc, values, inv, normed_t, upstream, d_attn, x_t, q_t, k_t,
    spread_v, spread_o, pick_v, pick_o, mate_v, mate_o,
    state_own, state_sib, state_chip, state_far,
    later_own, later_sib, later_chip, later_far,
    part_o, sib_o, sum_o, far_o, own_o, part_v, sib_v, sum_v, far_v,
    load_sem, send_sem, recv_sem, spread_send, spread_recv, mate_send, mate_recv, ready,
):
    rep = lax.axis_index("rep")
    me = lax.axis_index("seq")
    core = lax.rem(me, 2)
    chip = me // 2
    sib = chip * 2 + 1 - core
    far = (1 - chip) * 2 + core
    diag = (1 - chip) * 2 + 1 - core
    positions, depth = x.shape
    width = q.shape[1]
    half = positions // 2
    pairs = width // PAIR
    scale_value = depth ** (-0.5)
    scale_output = width ** (-0.5)
    used = [0]

    def remote(src, dst, target):
        index = used[0]
        used[0] += 1
        return pltpu.make_async_remote_copy(
            src_ref=src, dst_ref=dst, send_sem=send_sem.at[index], recv_sem=recv_sem.at[index],
            device_id={"seq": target}, device_id_type=pl.DeviceIdType.MESH,
        )

    barrier = pltpu.get_barrier_semaphore()

    def tell(semaphore, target):
        pl.semaphore_signal(semaphore, inc=1, device_id=target, device_id_type=pl.DeviceIdType.MESH)

    def tell_reps(semaphore):
        @pl.loop(1, reps)
        def _(step):
            tell(semaphore, {"rep": lax.rem(rep + step, reps)})

    tell(barrier, {"seq": far})

    @pl.when(core == 0)
    def _():
        tell(barrier, {"seq": sib})

    @pl.when(core == 1)
    def _():
        tell_reps(barrier)

    loads = [
        pltpu.make_async_copy(src, dst, load_sem.at[index])
        for index, (src, dst) in enumerate(
            ((q_hbm, q), (k_hbm, k), (wv_hbm, wv.at[me]), (x_hbm, x), (wo_hbm, wo.at[me]), (c_hbm, c))
        )
    ]
    for copy in loads:
        copy.start()
    def split(rows, count=CHUNKS):
        return [pl.ds(i * (rows // count), rows // count) for i in range(count)]

    rows_v = split(wv.shape[1])
    first_o = wo.shape[1] * 7 // 16
    rows_o = [pl.ds(0, first_o), pl.ds(first_o, wo.shape[1] - first_o)]
    far_wv = [remote(wv_hbm.at[r], wv.at[me, r], far) for r in rows_v]
    sib_wv = remote(wv_hbm, wv.at[me], sib)
    far_wo = [remote(wo_hbm.at[r], wo.at[me, r], far) for r in rows_o]
    sib_wo = remote(wo_hbm, wo.at[me], sib)
    pass_wv = [remote(wv.at[far, r], wv.at[far, r], sib) for r in rows_v]
    pass_wo = [remote(wo.at[far, r], wo.at[far, r], sib) for r in rows_o]
    early = far_wv + far_wo[:1]

    @pl.when(core == 0)
    def _():
        pl.semaphore_wait(barrier, 1)
        for copy in early:
            copy.start()
        pl.semaphore_wait(ready.at[0], 1)

    @pl.when(core == 1)
    def _():
        pl.semaphore_wait(barrier, reps + 1)
        for copy in early:
            copy.start()
        tell(ready.at[0], {"seq": sib})
        tell_reps(ready.at[1])

    sib_wv.start()
    sib_wo.start()

    col_parts = reps // row_parts
    high_v, wide_v = spread_v.shape[1:]
    high_o, wide_o = spread_o.shape[1:]

    def place(index, high, wide):
        row = pl.multiple_of((index // col_parts) * high, high)
        column = pl.multiple_of(lax.rem(index, col_parts) * wide, wide)
        return pl.ds(row, high), pl.ds(column, wide)

    def piece(ref, index, high, wide):
        rows, columns = place(index, high, wide)
        return ref.at[rows, columns]

    sources = (sv_hbm, so_hbm)
    spreads = (spread_v, spread_o)
    picks = (pick_v, pick_o)
    mates = (mate_v, mate_o)
    extents = ((high_v, wide_v), (high_o, wide_o))

    side = reps // 2
    high, low = rep // side, lax.rem(rep, side)

    def exchange(step, kind, which):
        near = step // side
        group = high * near + (1 - high) * (1 - near)
        hop = step - near * (side - 1)
        target = group * side + lax.rem(low // 2 + hop // 2, side // 2) * 2 + lax.rem(low + hop, 2)
        if which == 0:
            src, dst = piece(sources[kind], target, *extents[kind]), spreads[kind]
            sems = (spread_send, spread_recv)
        else:
            src, dst = picks[kind].at[target], mates[kind]
            sems = (mate_send, mate_recv)
        return pltpu.make_async_remote_copy(
            src_ref=src, dst_ref=dst.at[rep], send_sem=sems[0].at[kind, step],
            recv_sem=sems[1].at[kind, step], device_id={"rep": target},
            device_id_type=pl.DeviceIdType.MESH,
        )

    def sender(step):
        near = step // side
        group = high * near + (1 - high) * (1 - near)
        hop = step - near * (side - 1)
        pair = lax.rem(low // 2 + side // 2 - hop // 2, side // 2)
        return group * side + pair * 2 + lax.rem(low + hop, 2)

    def run_exchange(kind, which, act):
        @pl.loop(0, reps - 1)
        def _(step):
            act(exchange(step, kind, which))

    @pl.when(core == 0)
    def _():
        pl.semaphore_wait(ready.at[2], 1)

    run_exchange(0, 0, lambda copy: copy.start())
    run_exchange(1, 0, lambda copy: copy.start())

    @pl.when(core == 1)
    def _():
        pl.semaphore_wait(ready.at[1], reps - 1)
        tell(ready.at[2], {"seq": sib})

    own_pieces = [
        pltpu.make_async_copy(piece(sv_hbm, rep, high_v, wide_v), spread_v.at[rep], load_sem.at[6]),
        pltpu.make_async_copy(piece(so_hbm, rep, high_o, wide_o), spread_o.at[rep], load_sem.at[7]),
    ]
    for copy in own_pieces:
        copy.start()

    mate = partner[rep]

    def pick(kind):
        own_pieces[kind].wait()
        run_exchange(kind, 0, lambda copy: copy.wait())

        @pl.loop(0, reps)
        def _(r):
            picks[kind][r] = spreads[kind][partner[r]]

        run_exchange(kind, 1, lambda copy: copy.start())
        mates[kind][rep] = spreads[kind][mate]

    def lanes(p):
        return pl.ds(pl.multiple_of(p * PAIR, PAIR), PAIR)

    def first_lanes(rows):
        return lax.broadcasted_iota(jnp.int32, (rows, PAIR), 1) < HEAD

    def diagonal():
        row = lax.broadcasted_iota(jnp.int32, (PAIR, PAIR), 0) < HEAD
        column = lax.broadcasted_iota(jnp.int32, (PAIR, PAIR), 1) < HEAD
        return row == column

    loads[0].wait()
    loads[1].wait()

    @pl.loop(0, pairs)
    def _(p):
        keys = k[:, lanes(p)]
        queries = q[:, lanes(p)]
        first = first_lanes(positions)
        zero = jnp.zeros_like(queries)
        causal = lax.broadcasted_iota(jnp.int32, (half, half), 0) >= lax.broadcasted_iota(
            jnp.int32, (half, half), 1
        )
        for h in range(2):
            mine = jnp.where(first, queries, zero) if h == 0 else jnp.where(first, zero, queries)
            head = p * 2 + h
            low = dot(mine[half:], keys[:half], NT)
            scores[head, half:, :half] = low.astype(BF16)
            for b in range(2):
                block = slice(b * half, (b + 1) * half)
                square = dot(mine[block], keys[block], NT)
                scores[head, block, block] = jnp.where(causal, square, 0.0).astype(BF16)

    tile = 256

    def add_values(block, begin):
        columns = pl.ds(pl.multiple_of(block * wv.shape[1], wv.shape[1]), wv.shape[1])

        @pl.loop(0, width // tile)
        def _(n):
            out = pl.ds(pl.multiple_of(n * tile, tile), tile)
            term = dot(x[:, columns], wv[block, :, out])
            acc[:, out] = term if begin else acc[:, out] + term

    def add_upstream(block):
        rows = wo.shape[1]
        upstream[:, pl.ds(pl.multiple_of(block * rows, rows), rows)] = (
            dot(c[...], wo[block], NT) * scale_output
        )

    loads[2].wait()
    loads[3].wait()
    add_values(me, True)
    sib_wv.wait()
    add_values(sib, False)
    loads[4].wait()
    loads[5].wait()
    add_upstream(me)
    sib_wo.wait()
    add_upstream(sib)
    def turn(array, turned):
        @pl.loop(0, array.shape[1] // PAIR)
        def _(p):
            turned[lanes(p), :] = array[:, lanes(p)].T

    turn(k, k_t)
    turn(x, x_t)
    turn(q, q_t)
    for arrive, forward in zip(far_wv, pass_wv):
        arrive.wait()
        forward.start()
    add_values(far, False)
    for forward in pass_wv:
        forward.wait()
    last = pl.ds(pl.multiple_of(diag * wv.shape[1], wv.shape[1]), wv.shape[1])

    @pl.loop(0, width // tile)
    def _(n):
        out = pl.ds(pl.multiple_of(n * tile, tile), tile)
        values[:, out] = ((acc[:, out] + dot(x[:, last], wv[diag, :, out])) * scale_value).astype(BF16)

    def states(left, right, own):
        @pl.loop(0, pairs // 2, unroll=True)
        def _(j):
            same = diagonal()
            terms = [
                dot(left[lanes(2 * j + i), :], right[:, lanes(2 * j + i)]) for i in range(2)
            ]
            own[j] = jnp.where(same, terms[0], pltpu.roll(jnp.where(same, terms[1], 0.0), HEAD, 1))

    def unpack(packed, i):
        same = diagonal()
        if i == 0:
            return jnp.where(same, packed, 0.0)
        return pltpu.roll(jnp.where(same, 0.0, packed), HEAD, 1)

    def chip_share(total, landed, sender):
        count = total.shape[0] // 2
        mine = pl.ds(core * count, count)
        cross = remote(total.at[mine], landed.at[mine], far)
        across = remote(landed.at[mine], landed.at[mine], sib)

        def start():
            @pl.when(chip == sender)
            def _():
                landed[...] = jnp.zeros_like(landed)
                cross.start()

        def wait():
            @pl.when(chip == sender)
            def _():
                cross.wait_send()

            @pl.when(chip != sender)
            def _():
                cross.wait_recv()
                across.start()
                across.wait()

        return start, wait

    states(k_t, values, state_own)
    to_sib = remote(state_own, state_sib, sib)
    to_far = chip_share(state_chip, state_far, 0)
    to_sib.start()
    to_sib.wait()
    state_chip[...] = (state_own[...] + state_sib[...]).astype(BF16)
    to_far[0]()
    far_wo[1].start()

    @pl.loop(0, pairs // 2)
    def _(p2):
        for i in range(2):
            p = p2 * 2 + i
            right = values[:, lanes(p)]
            first = first_lanes(half)
            for b in range(2):
                rows = slice(b * half, (b + 1) * half)
                both = [dot(scores[p * 2 + h, rows, : (b + 1) * half], right[: (b + 1) * half]) for h in range(2)]
                acc[rows, lanes(p)] = jnp.where(first, both[0], both[1])

    to_far[1]()
    after_core = (core == 1).astype(F32)
    after_chip = (chip == 1).astype(F32)

    def head_mean(array):
        ones = jnp.where(diagonal(), 1.0, 0.0).astype(BF16)
        top = array.astype(BF16)
        rest = (array - top.astype(F32)).astype(BF16)
        return (dot(top, ones) + dot(rest, ones)) * (1.0 / HEAD)

    @pl.loop(0, pairs // 2)
    def _(j):
        packed = after_core * state_sib[j] + after_chip * state_far[j].astype(F32)
        for i in range(2):
            span = lanes(2 * j + i)
            prior = unpack(packed, i).astype(BF16)
            attn = acc[:, span] + dot(q[:, span], prior)
            inverse = lax.rsqrt(head_mean(attn * attn) + norm_eps)
            unit = attn * inverse
            acc[:, span] = unit
            inv[:, span] = inverse
            normed_t[span, :] = unit.astype(BF16).T

    def tile_o(slot, dest):
        rows = part_o.shape[1]
        left = normed_t[pl.ds(pl.multiple_of(dest * rows, rows), rows), :]
        step = depth // 4

        @pl.loop(0, 4)
        def _(n):
            out = pl.ds(pl.multiple_of(n * step, step), step)
            part_o[slot, :, out] = (dot(left, c[:, out]) * scale_output).astype(BF16)

    def tile_v(slot, dest):
        rows = part_v.shape[1]

        @pl.loop(0, width // tile)
        def _(n):
            out = pl.ds(pl.multiple_of(n * tile, tile), tile)
            left = x_t[pl.ds(pl.multiple_of(dest * rows, rows), rows), :]
            part_v[slot, :, out] = (dot(left, values[:, out]) * scale_value).astype(BF16)

    def scatter(make_tile, part, from_sib, total, landed, count):
        rows = split(part.shape[1], count)
        pair_far = remote(part.at[0], from_sib.at[0], sib)
        pair_near = remote(part.at[2], from_sib.at[1], sib)
        cross = [remote(total.at[r], landed.at[r], far) for r in rows]
        make_tile(0, diag)
        pair_far.start()
        make_tile(1, far)
        pair_far.wait()
        total[...] = (part[1].astype(F32) + from_sib[0].astype(F32)).astype(BF16)
        return pair_near, cross

    near_o, cross_o = scatter(tile_o, part_o, sib_o, sum_o, far_o, CHUNKS)
    cross_o[0].start()
    pick(0)
    for arrive, forward in zip(far_wo, pass_wo):
        arrive.wait()
        forward.start()
    add_upstream(far)
    for forward in pass_wo:
        forward.wait()
    add_upstream(diag)

    @pl.loop(0, pairs)
    def _(p):
        span = lanes(p)
        up = upstream[:, span]
        unit = acc[:, span]
        d_attn[:, span] = (inv[:, span] * (up - unit * head_mean(unit * up))).astype(BF16)

    states(q_t, d_attn, later_own)
    later_to_sib = remote(later_own, later_sib, sib)
    later_to_far = chip_share(later_chip, later_far, 1)
    later_to_sib.start()
    later_to_sib.wait()
    later_chip[...] = (later_own[...] + later_sib[...]).astype(BF16)
    later_to_far[0]()
    cross_o[1].start()

    @pl.loop(0, pairs)
    def _(p):
        right = d_attn[:, lanes(p)]
        first = first_lanes(half)
        for b in range(2):
            rows = slice(b * half, (b + 1) * half)
            both = [dot(scores[p * 2 + h, b * half :, rows], right[b * half :], TN) for h in range(2)]
            acc[rows, lanes(p)] = jnp.where(first, both[0], both[1])

    pick(1)
    later_to_far[1]()
    before_core = (core == 0).astype(F32)
    before_chip = (chip == 0).astype(F32)

    @pl.loop(0, pairs // 2)
    def _(j):
        packed = before_core * later_sib[j] + before_chip * later_far[j].astype(F32)
        for i in range(2):
            span = lanes(2 * j + i)
            later = unpack(packed, i).astype(BF16)
            values[:, span] = (acc[:, span] + dot(k[:, span], later)).astype(BF16)

    near_v, cross_v = scatter(tile_v, part_v, sib_v, sum_v, far_v, 2 * CHUNKS)
    for copy in cross_v:
        copy.start()
    tile_o(2, sib)
    near_o.start()
    tile_o(3, me)
    tile_v(2, sib)
    near_v.start()
    tile_v(3, me)

    own_count = counts[rep].astype(F32)
    mate_count = counts[mate].astype(F32)
    share = jnp.full((1, 128), mate_count, F32) / jnp.full((1, 128), own_count + mate_count, F32)
    mix = share[0:1, 0:1]

    run_exchange(0, 1, lambda copy: copy.wait())
    near_v.wait()

    def finish(out, weight, theirs, part, from_sib, landed, high, wide, index):
        at = place(index, high, wide)
        grad = part[(3, *at)].astype(F32) + from_sib[(1, *at)].astype(F32) + landed[at].astype(F32)
        mixed = (1.0 - mix) * weight[(me, *at)].astype(F32) + mix * theirs[index].astype(F32)
        out[at] = (mixed - learning_rate * grad).astype(BF16)

    def finish_o(index):
        at = place(index, high_o, wide_o)
        no_ref[at] = (own_o[at] + mix * mates[1][index].astype(F32)).astype(BF16)

    near_o.wait()
    for copy in cross_o:
        copy.wait()

    @pl.loop(0, reps)
    def _(index):
        at = place(index, high_o, wide_o)
        grad = part_o[(3, *at)].astype(F32) + sib_o[(1, *at)].astype(F32) + far_o[at].astype(F32)
        own_o[at] = (1.0 - mix) * wo[(me, *at)].astype(F32) - learning_rate * grad

    finish_o(rep)
    parts_v = len(cross_v)
    for i, copy in enumerate(cross_v):
        copy.wait()

        @pl.loop(i * reps // parts_v, (i + 1) * reps // parts_v)
        def _(index):
            finish(nv_ref, wv, mates[0], part_v, sib_v, far_v, high_v, wide_v, index)

    @pl.loop(0, reps - 1)
    def _(step):
        exchange(step, 1, 1).wait()
        finish_o(sender(step))


def hand_over(*refs):
    sources, results, sems = refs[:2], refs[2:4], refs[4]
    copies = []
    for kind in range(2):
        step = sources[kind].shape[0] // CHUNKS
        for i in range(CHUNKS):
            rows = pl.ds(i * step, step)
            copies.append(pltpu.make_async_copy(sources[kind].at[rows], results[kind].at[rows], sems.at[kind * CHUNKS + i]))
    for copy in copies:
        copy.start()
    for copy in copies:
        copy.wait()


def on_device(
    inputs, query, key_feat, cotangent, value_weight, output_weight, stale_value, stale_output,
    step_counts, partner,
):
    arrays = [
        a[0] for a in (inputs, query, key_feat, cotangent, value_weight, output_weight, stale_value, stale_output)
    ]
    reps = lax.axis_size("rep")
    seqs = lax.axis_size("seq")
    positions, depth = arrays[0].shape
    width = arrays[1].shape[1]
    rows_v, rows_o = arrays[4].shape[0], arrays[5].shape[0]
    row_parts = min(reps, 8)
    col_parts = reps // row_parts
    piece_v = (reps, rows_v // row_parts, width // col_parts)
    piece_o = (reps, rows_o // row_parts, depth // col_parts)
    packed = (width // PAIR // 2, PAIR, PAIR)
    vmem = pltpu.VMEM
    scratch = [
        vmem((positions, depth), BF16),
        vmem((positions, width), BF16),
        vmem((positions, width), BF16),
        vmem((positions, depth), BF16),
        vmem((seqs, rows_v, width), BF16),
        vmem((seqs, rows_o, depth), BF16),
        vmem((width // HEAD, positions, positions), BF16),
        vmem((positions, width), F32),
        vmem((positions, width), BF16),
        vmem((positions, width), F32),
        vmem((width, positions), BF16),
        vmem((positions, width), F32),
        vmem((positions, width), BF16),
        vmem((depth, positions), BF16),
        vmem((width, positions), BF16),
        vmem((width, positions), BF16),
        vmem(piece_v, BF16), vmem(piece_o, BF16),
        vmem(piece_v, BF16), vmem(piece_o, BF16),
        vmem(piece_v, BF16), vmem(piece_o, BF16),
        vmem(packed, F32), vmem(packed, F32), vmem(packed, BF16), vmem(packed, BF16),
        vmem(packed, F32), vmem(packed, F32), vmem(packed, BF16), vmem(packed, BF16),
        vmem((4, rows_o, depth), BF16), vmem((2, rows_o, depth), BF16),
        vmem((rows_o, depth), BF16), vmem((rows_o, depth), BF16), vmem((rows_o, depth), F32),
        vmem((4, rows_v, width), BF16), vmem((2, rows_v, width), BF16),
        vmem((rows_v, width), BF16), vmem((rows_v, width), BF16),
        pltpu.SemaphoreType.DMA((8,)),
        pltpu.SemaphoreType.DMA((26,)),
        pltpu.SemaphoreType.DMA((26,)),
        pltpu.SemaphoreType.DMA((2, reps)),
        pltpu.SemaphoreType.DMA((2, reps)),
        pltpu.SemaphoreType.DMA((2, reps)),
        pltpu.SemaphoreType.DMA((2, reps)),
        pltpu.SemaphoreType.REGULAR((3,)),
    ]
    outs = pl.pallas_call(
        functools.partial(kernel, reps, row_parts),
        out_shape=(vmem((rows_v, width), BF16), vmem((rows_o, depth), BF16)),
        in_specs=[pl.BlockSpec(memory_space=pl.ANY)] * 8
        + [pl.BlockSpec(memory_space=pltpu.SMEM)] * 2,
        out_specs=(pl.BlockSpec(memory_space=vmem), pl.BlockSpec(memory_space=vmem)),
        scratch_shapes=scratch,
        compiler_params=pltpu.CompilerParams(
            collective_id=0, has_side_effects=True, vmem_limit_bytes=64749568
        ),
        name="gossip_step",
    )(*arrays, step_counts, partner)
    whole = pl.BlockSpec(memory_space=pl.ANY)
    outs = [pltpu.with_memory_space_constraint(out, pltpu.VMEM) for out in outs]
    outs = pl.pallas_call(
        hand_over,
        out_shape=tuple(jax.ShapeDtypeStruct(out.shape, BF16) for out in outs),
        in_specs=[pl.BlockSpec(memory_space=vmem)] * 2,
        out_specs=(whole, whole),
        scratch_shapes=[pltpu.SemaphoreType.DMA((2 * CHUNKS,))],
        compiler_params=pltpu.CompilerParams(vmem_limit_bytes=2**20),
        name="hand_over",
    )(*outs)
    return outs[0][None], outs[1][None]


def solution(mesh):
    placed = (P("rep", "seq", None),) * 8 + (P(), P())
    return jax.shard_map(
        on_device,
        mesh=mesh,
        in_specs=placed,
        out_specs=(P("rep", "seq", None), P("rep", "seq", None)),
        check_vma=False,
    )
```

```python
import functools

import jax
import jax.numpy as jnp
from jax import lax
from jax.experimental import pallas as pl
from jax.experimental.pallas import tpu as pltpu
from jax.sharding import PartitionSpec as P

HEAD = 64
PAIR = 2 * HEAD
learning_rate = 0.25
norm_eps = 1e-06
F32 = jnp.float32
BF16 = jnp.bfloat16
TN = (((0,), (0,)), ((), ()))
NT = (((1,), (1,)), ((), ()))
CHUNKS = 2


def dot(a, b, dims=(((1,), (0,)), ((), ()))):
    return lax.dot_general(a, b, dims, preferred_element_type=F32)


def kernel(
    reps, row_parts,
    x_hbm, q_hbm, k_hbm, c_hbm, wv_hbm, wo_hbm, sv_hbm, so_hbm, counts, partner,
    nv_ref, no_ref,
    x, q, k, c, wv, wo, scores, acc, values, inv, normed_t, upstream, d_attn, x_t, q_t, k_t,
    spread_v, spread_o, pick_v, pick_o, mate_v, mate_o,
    state_own, state_sib, state_chip, state_far,
    later_own, later_sib, later_chip, later_far,
    part_o, sib_o, sum_o, far_o, own_o, part_v, sib_v, sum_v, far_v,
    load_sem, send_sem, recv_sem, spread_send, spread_recv, mate_send, mate_recv, ready,
):
    rep = lax.axis_index("rep")
    me = lax.axis_index("seq")
    core = lax.rem(me, 2)
    chip = me // 2
    sib = chip * 2 + 1 - core
    far = (1 - chip) * 2 + core
    diag = (1 - chip) * 2 + 1 - core
    positions, depth = x.shape
    width = q.shape[1]
    half = positions // 2
    pairs = width // PAIR
    scale_value = depth ** (-0.5)
    scale_output = width ** (-0.5)
    used = [0]

    def remote(src, dst, target):
        index = used[0]
        used[0] += 1
        return pltpu.make_async_remote_copy(
            src_ref=src, dst_ref=dst, send_sem=send_sem.at[index], recv_sem=recv_sem.at[index],
            device_id={"seq": target}, device_id_type=pl.DeviceIdType.MESH,
        )

    barrier = pltpu.get_barrier_semaphore()

    def tell(semaphore, target):
        pl.semaphore_signal(semaphore, inc=1, device_id=target, device_id_type=pl.DeviceIdType.MESH)

    def tell_reps(semaphore):
        @pl.loop(1, reps)
        def _(step):
            tell(semaphore, {"rep": lax.rem(rep + step, reps)})

    tell(barrier, {"seq": far})

    @pl.when(core == 0)
    def _():
        tell(barrier, {"seq": sib})

    @pl.when(core == 1)
    def _():
        tell_reps(barrier)

    loads = [
        pltpu.make_async_copy(src, dst, load_sem.at[index])
        for index, (src, dst) in enumerate(
            ((q_hbm, q), (k_hbm, k), (wv_hbm, wv.at[me]), (x_hbm, x), (wo_hbm, wo.at[me]), (c_hbm, c))
        )
    ]
    for copy in loads:
        copy.start()
    def split(rows, count=CHUNKS):
        return [pl.ds(i * (rows // count), rows // count) for i in range(count)]

    rows_v = split(wv.shape[1])
    first_o = wo.shape[1] * 7 // 16
    rows_o = [pl.ds(0, first_o), pl.ds(first_o, wo.shape[1] - first_o)]
    far_wv = [remote(wv_hbm.at[r], wv.at[me, r], far) for r in rows_v]
    sib_wv = remote(wv_hbm, wv.at[me], sib)
    far_wo = [remote(wo_hbm.at[r], wo.at[me, r], far) for r in rows_o]
    sib_wo = remote(wo_hbm, wo.at[me], sib)
    pass_wv = [remote(wv.at[far, r], wv.at[far, r], sib) for r in rows_v]
    pass_wo = [remote(wo.at[far, r], wo.at[far, r], sib) for r in rows_o]
    early = far_wv + far_wo[:1]

    @pl.when(core == 0)
    def _():
        pl.semaphore_wait(barrier, 1)
        for copy in early:
            copy.start()
        pl.semaphore_wait(ready.at[0], 1)

    @pl.when(core == 1)
    def _():
        pl.semaphore_wait(barrier, reps + 1)
        for copy in early:
            copy.start()
        tell(ready.at[0], {"seq": sib})
        tell_reps(ready.at[1])

    sib_wv.start()
    sib_wo.start()

    col_parts = reps // row_parts
    high_v, wide_v = spread_v.shape[1:]
    high_o, wide_o = spread_o.shape[1:]

    def place(index, high, wide):
        row = pl.multiple_of((index // col_parts) * high, high)
        column = pl.multiple_of(lax.rem(index, col_parts) * wide, wide)
        return pl.ds(row, high), pl.ds(column, wide)

    def piece(ref, index, high, wide):
        rows, columns = place(index, high, wide)
        return ref.at[rows, columns]

    sources = (sv_hbm, so_hbm)
    spreads = (spread_v, spread_o)
    picks = (pick_v, pick_o)
    mates = (mate_v, mate_o)
    extents = ((high_v, wide_v), (high_o, wide_o))

    side = reps // 2
    high, low = rep // side, lax.rem(rep, side)

    def exchange(step, kind, which):
        near = step // side
        group = high * near + (1 - high) * (1 - near)
        hop = step - near * (side - 1)
        target = group * side + lax.rem(low // 2 + hop // 2, side // 2) * 2 + lax.rem(low + hop, 2)
        if which == 0:
            src, dst = piece(sources[kind], target, *extents[kind]), spreads[kind]
            sems = (spread_send, spread_recv)
        else:
            src, dst = picks[kind].at[target], mates[kind]
            sems = (mate_send, mate_recv)
        return pltpu.make_async_remote_copy(
            src_ref=src, dst_ref=dst.at[rep], send_sem=sems[0].at[kind, step],
            recv_sem=sems[1].at[kind, step], device_id={"rep": target},
            device_id_type=pl.DeviceIdType.MESH,
        )

    def sender(step):
        near = step // side
        group = high * near + (1 - high) * (1 - near)
        hop = step - near * (side - 1)
        pair = lax.rem(low // 2 + side // 2 - hop // 2, side // 2)
        return group * side + pair * 2 + lax.rem(low + hop, 2)

    def run_exchange(kind, which, act):
        @pl.loop(0, reps - 1)
        def _(step):
            act(exchange(step, kind, which))

    @pl.when(core == 0)
    def _():
        pl.semaphore_wait(ready.at[2], 1)

    run_exchange(0, 0, lambda copy: copy.start())
    run_exchange(1, 0, lambda copy: copy.start())

    @pl.when(core == 1)
    def _():
        pl.semaphore_wait(ready.at[1], reps - 1)
        tell(ready.at[2], {"seq": sib})

    own_pieces = [
        pltpu.make_async_copy(piece(sv_hbm, rep, high_v, wide_v), spread_v.at[rep], load_sem.at[6]),
        pltpu.make_async_copy(piece(so_hbm, rep, high_o, wide_o), spread_o.at[rep], load_sem.at[7]),
    ]
    for copy in own_pieces:
        copy.start()

    mate = partner[rep]

    def pick(kind):
        own_pieces[kind].wait()
        run_exchange(kind, 0, lambda copy: copy.wait())

        @pl.loop(0, reps)
        def _(r):
            picks[kind][r] = spreads[kind][partner[r]]

        run_exchange(kind, 1, lambda copy: copy.start())
        mates[kind][rep] = spreads[kind][mate]

    def lanes(p):
        return pl.ds(pl.multiple_of(p * PAIR, PAIR), PAIR)

    def first_lanes(rows):
        return lax.broadcasted_iota(jnp.int32, (rows, PAIR), 1) < HEAD

    def diagonal():
        row = lax.broadcasted_iota(jnp.int32, (PAIR, PAIR), 0) < HEAD
        column = lax.broadcasted_iota(jnp.int32, (PAIR, PAIR), 1) < HEAD
        return row == column

    loads[0].wait()
    loads[1].wait()

    @pl.loop(0, pairs)
    def _(p):
        keys = k[:, lanes(p)]
        queries = q[:, lanes(p)]
        first = first_lanes(positions)
        zero = jnp.zeros_like(queries)
        causal = lax.broadcasted_iota(jnp.int32, (half, half), 0) >= lax.broadcasted_iota(
            jnp.int32, (half, half), 1
        )
        for h in range(2):
            mine = jnp.where(first, queries, zero) if h == 0 else jnp.where(first, zero, queries)
            head = p * 2 + h
            low = dot(mine[half:], keys[:half], NT)
            scores[head, half:, :half] = low.astype(BF16)
            for b in range(2):
                block = slice(b * half, (b + 1) * half)
                square = dot(mine[block], keys[block], NT)
                scores[head, block, block] = jnp.where(causal, square, 0.0).astype(BF16)

    tile = 256

    def add_values(block, begin):
        columns = pl.ds(pl.multiple_of(block * wv.shape[1], wv.shape[1]), wv.shape[1])

        @pl.loop(0, width // tile)
        def _(n):
            out = pl.ds(pl.multiple_of(n * tile, tile), tile)
            term = dot(x[:, columns], wv[block, :, out])
            acc[:, out] = term if begin else acc[:, out] + term

    def add_upstream(block):
        rows = wo.shape[1]
        upstream[:, pl.ds(pl.multiple_of(block * rows, rows), rows)] = (
            dot(c[...], wo[block], NT) * scale_output
        )

    loads[2].wait()
    loads[3].wait()
    add_values(me, True)
    sib_wv.wait()
    add_values(sib, False)
    loads[4].wait()
    loads[5].wait()
    add_upstream(me)
    sib_wo.wait()
    add_upstream(sib)
    def turn(array, turned):
        @pl.loop(0, array.shape[1] // PAIR)
        def _(p):
            turned[lanes(p), :] = array[:, lanes(p)].T

    turn(k, k_t)
    turn(x, x_t)
    turn(q, q_t)
    for arrive, forward in zip(far_wv, pass_wv):
        arrive.wait()
        forward.start()
    add_values(far, False)
    for forward in pass_wv:
        forward.wait()
    last = pl.ds(pl.multiple_of(diag * wv.shape[1], wv.shape[1]), wv.shape[1])

    @pl.loop(0, width // tile)
    def _(n):
        out = pl.ds(pl.multiple_of(n * tile, tile), tile)
        values[:, out] = ((acc[:, out] + dot(x[:, last], wv[diag, :, out])) * scale_value).astype(BF16)

    def states(left, right, own):
        @pl.loop(0, pairs // 2, unroll=True)
        def _(j):
            same = diagonal()
            terms = [
                dot(left[lanes(2 * j + i), :], right[:, lanes(2 * j + i)]) for i in range(2)
            ]
            own[j] = jnp.where(same, terms[0], pltpu.roll(jnp.where(same, terms[1], 0.0), HEAD, 1))

    def unpack(packed, i):
        same = diagonal()
        if i == 0:
            return jnp.where(same, packed, 0.0)
        return pltpu.roll(jnp.where(same, 0.0, packed), HEAD, 1)

    def chip_share(total, landed, sender):
        count = total.shape[0] // 2
        mine = pl.ds(core * count, count)
        cross = remote(total.at[mine], landed.at[mine], far)
        across = remote(landed.at[mine], landed.at[mine], sib)

        def start():
            @pl.when(chip == sender)
            def _():
                landed[...] = jnp.zeros_like(landed)
                cross.start()

        def wait():
            @pl.when(chip == sender)
            def _():
                cross.wait_send()

            @pl.when(chip != sender)
            def _():
                cross.wait_recv()
                across.start()
                across.wait()

        return start, wait

    states(k_t, values, state_own)
    to_sib = remote(state_own, state_sib, sib)
    to_far = chip_share(state_chip, state_far, 0)
    to_sib.start()
    to_sib.wait()
    state_chip[...] = (state_own[...] + state_sib[...]).astype(BF16)
    to_far[0]()
    far_wo[1].start()

    @pl.loop(0, pairs // 2)
    def _(p2):
        for i in range(2):
            p = p2 * 2 + i
            right = values[:, lanes(p)]
            first = first_lanes(half)
            for b in range(2):
                rows = slice(b * half, (b + 1) * half)
                both = [dot(scores[p * 2 + h, rows, : (b + 1) * half], right[: (b + 1) * half]) for h in range(2)]
                acc[rows, lanes(p)] = jnp.where(first, both[0], both[1])

    to_far[1]()
    after_core = (core == 1).astype(F32)
    after_chip = (chip == 1).astype(F32)

    def head_mean(array):
        ones = jnp.where(diagonal(), 1.0, 0.0).astype(BF16)
        top = array.astype(BF16)
        rest = (array - top.astype(F32)).astype(BF16)
        return (dot(top, ones) + dot(rest, ones)) * (1.0 / HEAD)

    @pl.loop(0, pairs // 2)
    def _(j):
        packed = after_core * state_sib[j] + after_chip * state_far[j].astype(F32)
        for i in range(2):
            span = lanes(2 * j + i)
            prior = unpack(packed, i).astype(BF16)
            attn = acc[:, span] + dot(q[:, span], prior)
            inverse = lax.rsqrt(head_mean(attn * attn) + norm_eps)
            unit = attn * inverse
            acc[:, span] = unit
            inv[:, span] = inverse
            normed_t[span, :] = unit.astype(BF16).T

    def tile_o(slot, dest):
        rows = part_o.shape[1]
        left = normed_t[pl.ds(pl.multiple_of(dest * rows, rows), rows), :]
        step = depth // 4

        @pl.loop(0, 4)
        def _(n):
            out = pl.ds(pl.multiple_of(n * step, step), step)
            part_o[slot, :, out] = (dot(left, c[:, out]) * scale_output).astype(BF16)

    def tile_v(slot, dest):
        rows = part_v.shape[1]

        @pl.loop(0, width // tile)
        def _(n):
            out = pl.ds(pl.multiple_of(n * tile, tile), tile)
            left = x_t[pl.ds(pl.multiple_of(dest * rows, rows), rows), :]
            part_v[slot, :, out] = (dot(left, values[:, out]) * scale_value).astype(BF16)

    def scatter(make_tile, part, from_sib, total, landed, count, begun):
        rows = split(part.shape[1], count)
        pair_far = remote(part.at[0], from_sib.at[0], sib)
        pair_near = remote(part.at[2], from_sib.at[1], sib)
        cross = [remote(total.at[r], landed.at[r], far) for r in rows]
        make_tile(0, diag)
        pair_far.start()
        make_tile(1, far)
        pair_far.wait()
        for i, r in enumerate(rows):
            total[r] = (part[1, r].astype(F32) + from_sib[0, r].astype(F32)).astype(BF16)
            if i < begun:
                cross[i].start()
        return pair_near, cross

    near_o, cross_o = scatter(tile_o, part_o, sib_o, sum_o, far_o, CHUNKS, 1)
    pick(0)
    for arrive, forward in zip(far_wo, pass_wo):
        arrive.wait()
        forward.start()
    add_upstream(far)
    for forward in pass_wo:
        forward.wait()
    add_upstream(diag)

    @pl.loop(0, pairs)
    def _(p):
        span = lanes(p)
        up = upstream[:, span]
        unit = acc[:, span]
        d_attn[:, span] = (inv[:, span] * (up - unit * head_mean(unit * up))).astype(BF16)

    states(q_t, d_attn, later_own)
    later_to_sib = remote(later_own, later_sib, sib)
    later_to_far = chip_share(later_chip, later_far, 1)
    later_to_sib.start()
    later_to_sib.wait()
    later_chip[...] = (later_own[...] + later_sib[...]).astype(BF16)
    later_to_far[0]()
    cross_o[1].start()

    @pl.loop(0, pairs)
    def _(p):
        right = d_attn[:, lanes(p)]
        first = first_lanes(half)
        for b in range(2):
            rows = slice(b * half, (b + 1) * half)
            both = [dot(scores[p * 2 + h, b * half :, rows], right[b * half :], TN) for h in range(2)]
            acc[rows, lanes(p)] = jnp.where(first, both[0], both[1])

    later_to_far[1]()
    before_core = (core == 0).astype(F32)
    before_chip = (chip == 0).astype(F32)

    @pl.loop(0, pairs // 2)
    def _(j):
        packed = before_core * later_sib[j] + before_chip * later_far[j].astype(F32)
        for i in range(2):
            span = lanes(2 * j + i)
            later = unpack(packed, i).astype(BF16)
            values[:, span] = (acc[:, span] + dot(k[:, span], later)).astype(BF16)

    pick(1)
    near_v, cross_v = scatter(tile_v, part_v, sib_v, sum_v, far_v, 2 * CHUNKS, 2 * CHUNKS)
    tile_o(2, sib)
    near_o.start()
    tile_o(3, me)
    tile_v(2, sib)
    near_v.start()
    tile_v(3, me)

    own_count = counts[rep].astype(F32)
    mate_count = counts[mate].astype(F32)
    share = jnp.full((1, 128), mate_count, F32) / jnp.full((1, 128), own_count + mate_count, F32)
    mix = share[0:1, 0:1]

    run_exchange(0, 1, lambda copy: copy.wait())
    near_v.wait()

    def finish(out, weight, theirs, part, from_sib, landed, high, wide, index):
        at = place(index, high, wide)
        grad = part[(3, *at)].astype(F32) + from_sib[(1, *at)].astype(F32) + landed[at].astype(F32)
        mixed = (1.0 - mix) * weight[(me, *at)].astype(F32) + mix * theirs[index].astype(F32)
        out[at] = (mixed - learning_rate * grad).astype(BF16)

    def finish_o(index):
        at = place(index, high_o, wide_o)
        no_ref[at] = (own_o[at] + mix * mates[1][index].astype(F32)).astype(BF16)

    near_o.wait()
    for copy in cross_o:
        copy.wait()

    @pl.loop(0, reps)
    def _(index):
        at = place(index, high_o, wide_o)
        grad = part_o[(3, *at)].astype(F32) + sib_o[(1, *at)].astype(F32) + far_o[at].astype(F32)
        own_o[at] = (1.0 - mix) * wo[(me, *at)].astype(F32) - learning_rate * grad

    finish_o(rep)
    parts_v = len(cross_v)
    for i, copy in enumerate(cross_v):
        copy.wait()

        @pl.loop(i * reps // parts_v, (i + 1) * reps // parts_v)
        def _(index):
            finish(nv_ref, wv, mates[0], part_v, sib_v, far_v, high_v, wide_v, index)

    @pl.loop(0, reps - 1)
    def _(step):
        exchange(step, 1, 1).wait()
        finish_o(sender(step))


def hand_over(*refs):
    sources, results, sems = refs[:2], refs[2:4], refs[4]
    copies = []
    for kind in range(2):
        step = sources[kind].shape[0] // CHUNKS
        for i in range(CHUNKS):
            rows = pl.ds(i * step, step)
            copies.append(pltpu.make_async_copy(sources[kind].at[rows], results[kind].at[rows], sems.at[kind * CHUNKS + i]))
    for copy in copies:
        copy.start()
    for copy in copies:
        copy.wait()


def on_device(
    inputs, query, key_feat, cotangent, value_weight, output_weight, stale_value, stale_output,
    step_counts, partner,
):
    arrays = [
        a[0] for a in (inputs, query, key_feat, cotangent, value_weight, output_weight, stale_value, stale_output)
    ]
    reps = lax.axis_size("rep")
    seqs = lax.axis_size("seq")
    positions, depth = arrays[0].shape
    width = arrays[1].shape[1]
    rows_v, rows_o = arrays[4].shape[0], arrays[5].shape[0]
    row_parts = min(reps, 8)
    col_parts = reps // row_parts
    piece_v = (reps, rows_v // row_parts, width // col_parts)
    piece_o = (reps, rows_o // row_parts, depth // col_parts)
    packed = (width // PAIR // 2, PAIR, PAIR)
    vmem = pltpu.VMEM
    scratch = [
        vmem((positions, depth), BF16),
        vmem((positions, width), BF16),
        vmem((positions, width), BF16),
        vmem((positions, depth), BF16),
        vmem((seqs, rows_v, width), BF16),
        vmem((seqs, rows_o, depth), BF16),
        vmem((width // HEAD, positions, positions), BF16),
        vmem((positions, width), F32),
        vmem((positions, width), BF16),
        vmem((positions, width), F32),
        vmem((width, positions), BF16),
        vmem((positions, width), F32),
        vmem((positions, width), BF16),
        vmem((depth, positions), BF16),
        vmem((width, positions), BF16),
        vmem((width, positions), BF16),
        vmem(piece_v, BF16), vmem(piece_o, BF16),
        vmem(piece_v, BF16), vmem(piece_o, BF16),
        vmem(piece_v, BF16), vmem(piece_o, BF16),
        vmem(packed, F32), vmem(packed, F32), vmem(packed, BF16), vmem(packed, BF16),
        vmem(packed, F32), vmem(packed, F32), vmem(packed, BF16), vmem(packed, BF16),
        vmem((4, rows_o, depth), BF16), vmem((2, rows_o, depth), BF16),
        vmem((rows_o, depth), BF16), vmem((rows_o, depth), BF16), vmem((rows_o, depth), F32),
        vmem((4, rows_v, width), BF16), vmem((2, rows_v, width), BF16),
        vmem((rows_v, width), BF16), vmem((rows_v, width), BF16),
        pltpu.SemaphoreType.DMA((8,)),
        pltpu.SemaphoreType.DMA((26,)),
        pltpu.SemaphoreType.DMA((26,)),
        pltpu.SemaphoreType.DMA((2, reps)),
        pltpu.SemaphoreType.DMA((2, reps)),
        pltpu.SemaphoreType.DMA((2, reps)),
        pltpu.SemaphoreType.DMA((2, reps)),
        pltpu.SemaphoreType.REGULAR((3,)),
    ]
    outs = pl.pallas_call(
        functools.partial(kernel, reps, row_parts),
        out_shape=(vmem((rows_v, width), BF16), vmem((rows_o, depth), BF16)),
        in_specs=[pl.BlockSpec(memory_space=pl.ANY)] * 8
        + [pl.BlockSpec(memory_space=pltpu.SMEM)] * 2,
        out_specs=(pl.BlockSpec(memory_space=vmem), pl.BlockSpec(memory_space=vmem)),
        scratch_shapes=scratch,
        compiler_params=pltpu.CompilerParams(
            collective_id=0, has_side_effects=True, vmem_limit_bytes=64749568
        ),
        name="gossip_step",
    )(*arrays, step_counts, partner)
    whole = pl.BlockSpec(memory_space=pl.ANY)
    outs = [pltpu.with_memory_space_constraint(out, pltpu.VMEM) for out in outs]
    outs = pl.pallas_call(
        hand_over,
        out_shape=tuple(jax.ShapeDtypeStruct(out.shape, BF16) for out in outs),
        in_specs=[pl.BlockSpec(memory_space=vmem)] * 2,
        out_specs=(whole, whole),
        scratch_shapes=[pltpu.SemaphoreType.DMA((2 * CHUNKS,))],
        compiler_params=pltpu.CompilerParams(vmem_limit_bytes=2**20),
        name="hand_over",
    )(*outs)
    return outs[0][None], outs[1][None]


def solution(mesh):
    placed = (P("rep", "seq", None),) * 8 + (P(), P())
    return jax.shard_map(
        on_device,
        mesh=mesh,
        in_specs=placed,
        out_specs=(P("rep", "seq", None), P("rep", "seq", None)),
        check_vma=False,
    )
```

```python
import functools

import jax
import jax.numpy as jnp
from jax import lax
from jax.experimental import pallas as pl
from jax.experimental.pallas import tpu as pltpu
from jax.sharding import PartitionSpec as P

HEAD = 64
PAIR = 2 * HEAD
learning_rate = 0.25
norm_eps = 1e-06
F32 = jnp.float32
BF16 = jnp.bfloat16
TN = (((0,), (0,)), ((), ()))
NT = (((1,), (1,)), ((), ()))
CHUNKS = 2


def dot(a, b, dims=(((1,), (0,)), ((), ()))):
    return lax.dot_general(a, b, dims, preferred_element_type=F32)


def kernel(
    reps, row_parts,
    x_hbm, q_hbm, k_hbm, c_hbm, wv_hbm, wo_hbm, sv_hbm, so_hbm, counts, partner,
    nv_ref, no_ref,
    x, q, k, c, wv, wo, scores, acc, values, inv, normed_t, upstream, d_attn, x_t, q_t, k_t,
    spread_v, spread_o, pick_v, pick_o, mate_v, mate_o,
    state_own, state_sib, state_chip, state_far,
    later_own, later_sib, later_chip, later_far,
    part_o, sib_o, sum_o, far_o, own_o, part_v, sib_v, sum_v, far_v,
    load_sem, send_sem, recv_sem, spread_send, spread_recv, mate_send, mate_recv, ready,
):
    rep = lax.axis_index("rep")
    me = lax.axis_index("seq")
    core = lax.rem(me, 2)
    chip = me // 2
    sib = chip * 2 + 1 - core
    far = (1 - chip) * 2 + core
    diag = (1 - chip) * 2 + 1 - core
    positions, depth = x.shape
    width = q.shape[1]
    half = positions // 2
    pairs = width // PAIR
    scale_value = depth ** (-0.5)
    scale_output = width ** (-0.5)
    used = [0]

    def remote(src, dst, target):
        index = used[0]
        used[0] += 1
        return pltpu.make_async_remote_copy(
            src_ref=src, dst_ref=dst, send_sem=send_sem.at[index], recv_sem=recv_sem.at[index],
            device_id={"seq": target}, device_id_type=pl.DeviceIdType.MESH,
        )

    barrier = pltpu.get_barrier_semaphore()

    def tell(semaphore, target):
        pl.semaphore_signal(semaphore, inc=1, device_id=target, device_id_type=pl.DeviceIdType.MESH)

    def tell_reps(semaphore):
        @pl.loop(1, reps)
        def _(step):
            tell(semaphore, {"rep": lax.rem(rep + step, reps)})

    tell(barrier, {"seq": far})

    @pl.when(core == 0)
    def _():
        tell(barrier, {"seq": sib})

    @pl.when(core == 1)
    def _():
        tell_reps(barrier)

    loads = [
        pltpu.make_async_copy(src, dst, load_sem.at[index])
        for index, (src, dst) in enumerate(
            ((q_hbm, q), (k_hbm, k), (wv_hbm, wv.at[me]), (x_hbm, x), (wo_hbm, wo.at[me]), (c_hbm, c))
        )
    ]
    for copy in loads:
        copy.start()
    def split(rows, count=CHUNKS):
        return [pl.ds(i * (rows // count), rows // count) for i in range(count)]

    rows_v = split(wv.shape[1])
    first_o = wo.shape[1] * 7 // 16
    rows_o = [pl.ds(0, first_o), pl.ds(first_o, wo.shape[1] - first_o)]
    far_wv = [remote(wv_hbm.at[r], wv.at[me, r], far) for r in rows_v]
    sib_wv = remote(wv_hbm, wv.at[me], sib)
    far_wo = [remote(wo_hbm.at[r], wo.at[me, r], far) for r in rows_o]
    sib_wo = remote(wo_hbm, wo.at[me], sib)
    pass_wv = [remote(wv.at[far, r], wv.at[far, r], sib) for r in rows_v]
    pass_wo = [remote(wo.at[far, r], wo.at[far, r], sib) for r in rows_o]
    early = far_wv + far_wo[:1]

    @pl.when(core == 0)
    def _():
        pl.semaphore_wait(barrier, 1)
        for copy in early:
            copy.start()
        pl.semaphore_wait(ready.at[0], 1)

    @pl.when(core == 1)
    def _():
        pl.semaphore_wait(barrier, reps + 1)
        for copy in early:
            copy.start()
        tell(ready.at[0], {"seq": sib})
        tell_reps(ready.at[1])

    sib_wv.start()
    sib_wo.start()

    col_parts = reps // row_parts
    high_v, wide_v = spread_v.shape[1:]
    high_o, wide_o = spread_o.shape[1:]

    def place(index, high, wide):
        row = pl.multiple_of((index // col_parts) * high, high)
        column = pl.multiple_of(lax.rem(index, col_parts) * wide, wide)
        return pl.ds(row, high), pl.ds(column, wide)

    def piece(ref, index, high, wide):
        rows, columns = place(index, high, wide)
        return ref.at[rows, columns]

    sources = (sv_hbm, so_hbm)
    spreads = (spread_v, spread_o)
    picks = (pick_v, pick_o)
    mates = (mate_v, mate_o)
    extents = ((high_v, wide_v), (high_o, wide_o))

    side = reps // 2
    high, low = rep // side, lax.rem(rep, side)

    def exchange(step, kind, which):
        near = step // side
        group = high * near + (1 - high) * (1 - near)
        hop = step - near * (side - 1)
        target = group * side + lax.rem(low // 2 + hop // 2, side // 2) * 2 + lax.rem(low + hop, 2)
        if which == 0:
            src, dst = piece(sources[kind], target, *extents[kind]), spreads[kind]
            sems = (spread_send, spread_recv)
        else:
            src, dst = picks[kind].at[target], mates[kind]
            sems = (mate_send, mate_recv)
        return pltpu.make_async_remote_copy(
            src_ref=src, dst_ref=dst.at[rep], send_sem=sems[0].at[kind, step],
            recv_sem=sems[1].at[kind, step], device_id={"rep": target},
            device_id_type=pl.DeviceIdType.MESH,
        )

    def sender(step):
        near = step // side
        group = high * near + (1 - high) * (1 - near)
        hop = step - near * (side - 1)
        pair = lax.rem(low // 2 + side // 2 - hop // 2, side // 2)
        return group * side + pair * 2 + lax.rem(low + hop, 2)

    def run_exchange(kind, which, act):
        @pl.loop(0, reps - 1)
        def _(step):
            act(exchange(step, kind, which))

    @pl.when(core == 0)
    def _():
        pl.semaphore_wait(ready.at[2], 1)

    run_exchange(0, 0, lambda copy: copy.start())
    run_exchange(1, 0, lambda copy: copy.start())

    @pl.when(core == 1)
    def _():
        pl.semaphore_wait(ready.at[1], reps - 1)
        tell(ready.at[2], {"seq": sib})

    own_pieces = [
        pltpu.make_async_copy(piece(sv_hbm, rep, high_v, wide_v), spread_v.at[rep], load_sem.at[6]),
        pltpu.make_async_copy(piece(so_hbm, rep, high_o, wide_o), spread_o.at[rep], load_sem.at[7]),
    ]
    for copy in own_pieces:
        copy.start()

    mate = partner[rep]

    def pick(kind):
        own_pieces[kind].wait()
        run_exchange(kind, 0, lambda copy: copy.wait())

        @pl.loop(0, reps)
        def _(r):
            picks[kind][r] = spreads[kind][partner[r]]

        run_exchange(kind, 1, lambda copy: copy.start())
        mates[kind][rep] = spreads[kind][mate]

    def lanes(p):
        return pl.ds(pl.multiple_of(p * PAIR, PAIR), PAIR)

    def first_lanes(rows):
        return lax.broadcasted_iota(jnp.int32, (rows, PAIR), 1) < HEAD

    def diagonal():
        row = lax.broadcasted_iota(jnp.int32, (PAIR, PAIR), 0) < HEAD
        column = lax.broadcasted_iota(jnp.int32, (PAIR, PAIR), 1) < HEAD
        return row == column

    loads[0].wait()
    loads[1].wait()

    @pl.loop(0, pairs)
    def _(p):
        keys = k[:, lanes(p)]
        queries = q[:, lanes(p)]
        first = first_lanes(positions)
        zero = jnp.zeros_like(queries)
        causal = lax.broadcasted_iota(jnp.int32, (half, half), 0) >= lax.broadcasted_iota(
            jnp.int32, (half, half), 1
        )
        for h in range(2):
            mine = jnp.where(first, queries, zero) if h == 0 else jnp.where(first, zero, queries)
            head = p * 2 + h
            low = dot(mine[half:], keys[:half], NT)
            scores[head, half:, :half] = low.astype(BF16)
            for b in range(2):
                block = slice(b * half, (b + 1) * half)
                square = dot(mine[block], keys[block], NT)
                scores[head, block, block] = jnp.where(causal, square, 0.0).astype(BF16)

    tile = 256

    def add_values(block, begin):
        columns = pl.ds(pl.multiple_of(block * wv.shape[1], wv.shape[1]), wv.shape[1])

        @pl.loop(0, width // tile)
        def _(n):
            out = pl.ds(pl.multiple_of(n * tile, tile), tile)
            term = dot(x[:, columns], wv[block, :, out])
            acc[:, out] = term if begin else acc[:, out] + term

    def add_upstream(block):
        rows = wo.shape[1]
        upstream[:, pl.ds(pl.multiple_of(block * rows, rows), rows)] = (
            dot(c[...], wo[block], NT) * scale_output
        )

    loads[2].wait()
    loads[3].wait()
    add_values(me, True)
    sib_wv.wait()
    add_values(sib, False)
    loads[4].wait()
    loads[5].wait()
    add_upstream(me)
    sib_wo.wait()
    add_upstream(sib)
    def turn(array, turned):
        @pl.loop(0, array.shape[1] // PAIR)
        def _(p):
            turned[lanes(p), :] = array[:, lanes(p)].T

    turn(k, k_t)
    turn(x, x_t)
    turn(q, q_t)
    for arrive, forward in zip(far_wv, pass_wv):
        arrive.wait()
        forward.start()
    add_values(far, False)
    for forward in pass_wv:
        forward.wait()
    last = pl.ds(pl.multiple_of(diag * wv.shape[1], wv.shape[1]), wv.shape[1])

    @pl.loop(0, width // tile)
    def _(n):
        out = pl.ds(pl.multiple_of(n * tile, tile), tile)
        values[:, out] = ((acc[:, out] + dot(x[:, last], wv[diag, :, out])) * scale_value).astype(BF16)

    def states(left, right, own):
        @pl.loop(0, pairs // 2, unroll=True)
        def _(j):
            same = diagonal()
            terms = [
                dot(left[lanes(2 * j + i), :], right[:, lanes(2 * j + i)]) for i in range(2)
            ]
            own[j] = jnp.where(same, terms[0], pltpu.roll(jnp.where(same, terms[1], 0.0), HEAD, 1))

    def unpack(packed, i):
        same = diagonal()
        if i == 0:
            return jnp.where(same, packed, 0.0)
        return pltpu.roll(jnp.where(same, 0.0, packed), HEAD, 1)

    def chip_share(total, landed, sender):
        count = total.shape[0] // 2
        mine = pl.ds(core * count, count)
        cross = remote(total.at[mine], landed.at[mine], far)
        across = remote(landed.at[mine], landed.at[mine], sib)

        def start():
            @pl.when(chip == sender)
            def _():
                landed[...] = jnp.zeros_like(landed)
                cross.start()

        def wait():
            @pl.when(chip == sender)
            def _():
                cross.wait_send()

            @pl.when(chip != sender)
            def _():
                cross.wait_recv()
                across.start()
                across.wait()

        return start, wait

    states(k_t, values, state_own)
    to_sib = remote(state_own, state_sib, sib)
    to_far = chip_share(state_chip, state_far, 0)
    to_sib.start()
    to_sib.wait()
    state_chip[...] = (state_own[...] + state_sib[...]).astype(BF16)
    to_far[0]()
    far_wo[1].start()

    @pl.loop(0, pairs // 2)
    def _(p2):
        for i in range(2):
            p = p2 * 2 + i
            right = values[:, lanes(p)]
            first = first_lanes(half)
            for b in range(2):
                rows = slice(b * half, (b + 1) * half)
                both = [dot(scores[p * 2 + h, rows, : (b + 1) * half], right[: (b + 1) * half]) for h in range(2)]
                acc[rows, lanes(p)] = jnp.where(first, both[0], both[1])

    to_far[1]()
    after_core = (core == 1).astype(F32)
    after_chip = (chip == 1).astype(F32)

    def head_mean(array):
        ones = jnp.where(diagonal(), 1.0, 0.0).astype(BF16)
        top = array.astype(BF16)
        rest = (array - top.astype(F32)).astype(BF16)
        return (dot(top, ones) + dot(rest, ones)) * (1.0 / HEAD)

    @pl.loop(0, pairs // 2)
    def _(j):
        packed = after_core * state_sib[j] + after_chip * state_far[j].astype(F32)
        for i in range(2):
            span = lanes(2 * j + i)
            prior = unpack(packed, i).astype(BF16)
            attn = acc[:, span] + dot(q[:, span], prior)
            inverse = lax.rsqrt(head_mean(attn * attn) + norm_eps)
            unit = attn * inverse
            acc[:, span] = unit
            inv[:, span] = inverse
            normed_t[span, :] = unit.astype(BF16).T

    def tile_o(slot, dest):
        rows = part_o.shape[1]
        left = normed_t[pl.ds(pl.multiple_of(dest * rows, rows), rows), :]
        step = depth // 4

        @pl.loop(0, 4)
        def _(n):
            out = pl.ds(pl.multiple_of(n * step, step), step)
            part_o[slot, :, out] = (dot(left, c[:, out]) * scale_output).astype(BF16)

    def tile_v(slot, dest):
        rows = part_v.shape[1]

        @pl.loop(0, width // tile)
        def _(n):
            out = pl.ds(pl.multiple_of(n * tile, tile), tile)
            left = x_t[pl.ds(pl.multiple_of(dest * rows, rows), rows), :]
            part_v[slot, :, out] = (dot(left, values[:, out]) * scale_value).astype(BF16)

    def scatter(make_tile, part, from_sib, total, landed, count, begun):
        rows = split(part.shape[1], count)
        pair_far = remote(part.at[0], from_sib.at[0], sib)
        pair_near = remote(part.at[2], from_sib.at[1], sib)
        cross = [remote(total.at[r], landed.at[r], far) for r in rows]
        make_tile(0, diag)
        pair_far.start()
        make_tile(1, far)
        pair_far.wait()
        for i, r in enumerate(rows):
            total[r] = (part[1, r].astype(F32) + from_sib[0, r].astype(F32)).astype(BF16)
            if i < begun:
                cross[i].start()
        return pair_near, cross

    near_o, cross_o = scatter(tile_o, part_o, sib_o, sum_o, far_o, CHUNKS, 1)
    pick(0)
    for arrive, forward in zip(far_wo, pass_wo):
        arrive.wait()
        forward.start()
    add_upstream(far)
    for forward in pass_wo:
        forward.wait()
    add_upstream(diag)

    @pl.loop(0, pairs)
    def _(p):
        span = lanes(p)
        up = upstream[:, span]
        unit = acc[:, span]
        d_attn[:, span] = (inv[:, span] * (up - unit * head_mean(unit * up))).astype(BF16)

    states(q_t, d_attn, later_own)
    later_to_sib = remote(later_own, later_sib, sib)
    later_to_far = chip_share(later_chip, later_far, 1)
    later_to_sib.start()
    later_to_sib.wait()
    later_chip[...] = (later_own[...] + later_sib[...]).astype(BF16)
    later_to_far[0]()
    cross_o[1].start()

    @pl.loop(0, pairs)
    def _(p):
        right = d_attn[:, lanes(p)]
        first = first_lanes(half)
        for b in range(2):
            rows = slice(b * half, (b + 1) * half)
            both = [dot(scores[p * 2 + h, b * half :, rows], right[b * half :], TN) for h in range(2)]
            acc[rows, lanes(p)] = jnp.where(first, both[0], both[1])

    later_to_far[1]()
    before_core = (core == 0).astype(F32)
    before_chip = (chip == 0).astype(F32)

    @pl.loop(0, pairs // 2)
    def _(j):
        packed = before_core * later_sib[j] + before_chip * later_far[j].astype(F32)
        for i in range(2):
            span = lanes(2 * j + i)
            later = unpack(packed, i).astype(BF16)
            values[:, span] = (acc[:, span] + dot(k[:, span], later)).astype(BF16)

    pick(1)
    near_v, cross_v = scatter(tile_v, part_v, sib_v, sum_v, far_v, 2 * CHUNKS, 2 * CHUNKS)
    tile_o(2, sib)
    near_o.start()
    tile_o(3, me)
    tile_v(2, sib)
    near_v.start()
    tile_v(3, me)

    own_count = counts[rep].astype(F32)
    mate_count = counts[mate].astype(F32)
    share = jnp.full((1, 128), mate_count, F32) / jnp.full((1, 128), own_count + mate_count, F32)
    mix = share[0:1, 0:1]

    run_exchange(0, 1, lambda copy: copy.wait())
    near_v.wait()

    def finish(out, weight, theirs, part, from_sib, landed, high, wide, index):
        at = place(index, high, wide)
        grad = part[(3, *at)].astype(F32) + from_sib[(1, *at)].astype(F32) + landed[at].astype(F32)
        mixed = (1.0 - mix) * weight[(me, *at)].astype(F32) + mix * theirs[index].astype(F32)
        out[at] = (mixed - learning_rate * grad).astype(BF16)

    def finish_o(index):
        at = place(index, high_o, wide_o)
        no_ref[at] = (own_o[at] + mix * mates[1][index].astype(F32)).astype(BF16)

    near_o.wait()
    for copy in cross_o:
        copy.wait()

    @pl.loop(0, reps)
    def _(index):
        at = place(index, high_o, wide_o)
        grad = part_o[(3, *at)].astype(F32) + sib_o[(1, *at)].astype(F32) + far_o[at].astype(F32)
        own_o[at] = (1.0 - mix) * wo[(me, *at)].astype(F32) - learning_rate * grad

    finish_o(rep)
    parts_v = len(cross_v)
    def finish_steps(begin, end):
        @pl.loop(begin, end)
        def _(step):
            exchange(step, 1, 1).wait()
            finish_o(sender(step))

    for i, copy in enumerate(cross_v):
        if i == parts_v - 1:
            finish_steps(0, side)
        copy.wait()

        @pl.loop(i * reps // parts_v, (i + 1) * reps // parts_v)
        def _(index):
            finish(nv_ref, wv, mates[0], part_v, sib_v, far_v, high_v, wide_v, index)

    finish_steps(side, reps - 1)


def hand_over(*refs):
    sources, results, sems = refs[:2], refs[2:4], refs[4]
    copies = []
    for kind in range(2):
        step = sources[kind].shape[0] // CHUNKS
        for i in range(CHUNKS):
            rows = pl.ds(i * step, step)
            copies.append(pltpu.make_async_copy(sources[kind].at[rows], results[kind].at[rows], sems.at[kind * CHUNKS + i]))
    for copy in copies:
        copy.start()
    for copy in copies:
        copy.wait()


def on_device(
    inputs, query, key_feat, cotangent, value_weight, output_weight, stale_value, stale_output,
    step_counts, partner,
):
    arrays = [
        a[0] for a in (inputs, query, key_feat, cotangent, value_weight, output_weight, stale_value, stale_output)
    ]
    reps = lax.axis_size("rep")
    seqs = lax.axis_size("seq")
    positions, depth = arrays[0].shape
    width = arrays[1].shape[1]
    rows_v, rows_o = arrays[4].shape[0], arrays[5].shape[0]
    row_parts = min(reps, 8)
    col_parts = reps // row_parts
    piece_v = (reps, rows_v // row_parts, width // col_parts)
    piece_o = (reps, rows_o // row_parts, depth // col_parts)
    packed = (width // PAIR // 2, PAIR, PAIR)
    vmem = pltpu.VMEM
    scratch = [
        vmem((positions, depth), BF16),
        vmem((positions, width), BF16),
        vmem((positions, width), BF16),
        vmem((positions, depth), BF16),
        vmem((seqs, rows_v, width), BF16),
        vmem((seqs, rows_o, depth), BF16),
        vmem((width // HEAD, positions, positions), BF16),
        vmem((positions, width), F32),
        vmem((positions, width), BF16),
        vmem((positions, width), F32),
        vmem((width, positions), BF16),
        vmem((positions, width), F32),
        vmem((positions, width), BF16),
        vmem((depth, positions), BF16),
        vmem((width, positions), BF16),
        vmem((width, positions), BF16),
        vmem(piece_v, BF16), vmem(piece_o, BF16),
        vmem(piece_v, BF16), vmem(piece_o, BF16),
        vmem(piece_v, BF16), vmem(piece_o, BF16),
        vmem(packed, F32), vmem(packed, F32), vmem(packed, BF16), vmem(packed, BF16),
        vmem(packed, F32), vmem(packed, F32), vmem(packed, BF16), vmem(packed, BF16),
        vmem((4, rows_o, depth), BF16), vmem((2, rows_o, depth), BF16),
        vmem((rows_o, depth), BF16), vmem((rows_o, depth), BF16), vmem((rows_o, depth), F32),
        vmem((4, rows_v, width), BF16), vmem((2, rows_v, width), BF16),
        vmem((rows_v, width), BF16), vmem((rows_v, width), BF16),
        pltpu.SemaphoreType.DMA((8,)),
        pltpu.SemaphoreType.DMA((26,)),
        pltpu.SemaphoreType.DMA((26,)),
        pltpu.SemaphoreType.DMA((2, reps)),
        pltpu.SemaphoreType.DMA((2, reps)),
        pltpu.SemaphoreType.DMA((2, reps)),
        pltpu.SemaphoreType.DMA((2, reps)),
        pltpu.SemaphoreType.REGULAR((3,)),
    ]
    outs = pl.pallas_call(
        functools.partial(kernel, reps, row_parts),
        out_shape=(vmem((rows_v, width), BF16), vmem((rows_o, depth), BF16)),
        in_specs=[pl.BlockSpec(memory_space=pl.ANY)] * 8
        + [pl.BlockSpec(memory_space=pltpu.SMEM)] * 2,
        out_specs=(pl.BlockSpec(memory_space=vmem), pl.BlockSpec(memory_space=vmem)),
        scratch_shapes=scratch,
        compiler_params=pltpu.CompilerParams(
            collective_id=0, has_side_effects=True, vmem_limit_bytes=64749568
        ),
        name="gossip_step",
    )(*arrays, step_counts, partner)
    whole = pl.BlockSpec(memory_space=pl.ANY)
    outs = [pltpu.with_memory_space_constraint(out, pltpu.VMEM) for out in outs]
    outs = pl.pallas_call(
        hand_over,
        out_shape=tuple(jax.ShapeDtypeStruct(out.shape, BF16) for out in outs),
        in_specs=[pl.BlockSpec(memory_space=vmem)] * 2,
        out_specs=(whole, whole),
        scratch_shapes=[pltpu.SemaphoreType.DMA((2 * CHUNKS,))],
        compiler_params=pltpu.CompilerParams(vmem_limit_bytes=2**20),
        name="hand_over",
    )(*outs)
    return outs[0][None], outs[1][None]


def solution(mesh):
    placed = (P("rep", "seq", None),) * 8 + (P(), P())
    return jax.shard_map(
        on_device,
        mesh=mesh,
        in_specs=placed,
        out_specs=(P("rep", "seq", None), P("rep", "seq", None)),
        check_vma=False,
    )
```
